32 devices in a mesh: fsdp: 8 (over y, x, core), mp: 4 (over z).
Axes of the slice: x: 2, y: 2, z: 4, core: 2. Of those that a mesh axis runs over, the one named last changes fastest.
Arguments:
- layer_input: float32 [4096, 768], P(('fsdp', 'mp')), may hold values from -6 to 6
- cotangent: float32 [4096, 768], P(('fsdp', 'mp')), may hold values from -6 to 6
- seq_lengths: int32 [4], replicated, may hold values from 1 to 2048, 4096 in all
- gain_attn: bfloat16 [768], P('fsdp'), may hold values from 0.5 to 1.5
- beta_attn: bfloat16 [768], P('fsdp'), may hold values from -3 to 3
- gain_mlp: bfloat16 [768], P('fsdp'), may hold values from 0.5 to 1.5
- beta_mlp: bfloat16 [768], P('fsdp'), may hold values from -3 to 3
- qkv_weight: bfloat16 [768, 3, 12, 64], P('fsdp'), may hold values from -0.21875 to 0.21875
- qkv_bias: bfloat16 [2304], P('fsdp'), may hold values from -3 to 3
- dense_weight: bfloat16 [768, 768], P(None, 'fsdp'), may hold values from -0.875 to 0.875
- dense_bias: bfloat16 [768], P('fsdp'), may hold values from -3 to 3
- up_weight: bfloat16 [768, 3072], P('fsdp', 'mp'), may hold values from -0.21875 to 0.21875
- up_bias: bfloat16 [3072], P('fsdp'), may hold values from -3 to 3
- down_weight: bfloat16 [768, 3072], P('fsdp', 'mp'), may hold values from -0.15625 to 0.15625
- down_bias: bfloat16 [768], P('fsdp'), may hold values from -3 to 3
Outputs:
- layer_output: float32 [4096, 768], P(('fsdp', 'mp'))
- input_grad: float32 [4096, 768], P(('fsdp', 'mp'))
- grad_qkv_weight: float32 [768, 3, 12, 64], P('fsdp')
- grad_qkv_bias: float32 [2304], P('fsdp')
- grad_dense_weight: float32 [768, 768], P(None, 'fsdp')
- grad_dense_bias: float32 [768], P('fsdp')
- grad_gain_attn: float32 [768], P('fsdp')
- grad_beta_attn: float32 [768], P('fsdp')
- grad_gain_mlp: float32 [768], P('fsdp')
- grad_beta_mlp: float32 [768], P('fsdp')
- grad_up_weight: float32 [768, 3072], P('fsdp', 'mp')
- grad_up_bias: float32 [3072], P('fsdp')
- grad_down_weight: float32 [768, 3072], P('fsdp', 'mp')
- grad_down_bias: float32 [768], P('fsdp')
The draws below stay inside these ranges and needn't reach their ends.
Inputs may be any that keep to these rules, and one draw needn't show every extreme that they name: `seq_lengths`: the longest sequence has exactly 2048 tokens; all lengths sum to 4096.
All inputs are finite; a program needn't handle non-finite values.
Results may differ from the reference program's by a relative error of at most 0.013.
Values may be sent and summed in bfloat16 or wider, within the bound.
A program may use at most 192 MiB of HBM per device.

```python
import math
import jax
import jax.numpy as jnp
import numpy as np
from jax import lax

D = 768
H = 12
HD = 64
ROT = 16
FF = 3072
TOKENS = 4096
MOST = 2048
SEQS = 4


def strengthened(array, key, source, target, parts, factor):
    def block_of(position):
        return (jnp.arange(array.shape[position]) // (array.shape[position] // parts)).reshape((-1,) + (1,) * (array.ndim - 1 - position))

    one_side = jax.random.permutation(key, parts)[block_of(target)]
    far = (block_of(target) + parts // 2) % parts
    return jnp.where((block_of(source) == one_side) | (block_of(source) == far), factor * array, array)


def block_levels(key, dims, split, low, top_value):
    loudness, own = 1.0, jax.random.fold_in(key, 6)
    for axis_at, shards_of in split:
        heights = jnp.exp(jax.random.uniform(jax.random.fold_in(own, axis_at), (shards_of,), jnp.float32, low / len(split), top_value / len(split)))
        loudness = loudness * jnp.repeat(heights, dims[axis_at] // shards_of).reshape([-1 if axis == axis_at else 1 for axis in range(len(dims))])
    return loudness


def split_up(number_of, total, bound, slope):
    loads = [(1 << 20) // math.isqrt(rank ** slope) + 1 for rank in range(2, number_of + 1)]
    spare, counts = total - bound - (number_of - 1), [1] * (number_of - 1)
    while spare > 0:
        candidates = [i for i in range(number_of - 1) if counts[i] < bound]
        mass, budget = sum([loads[i] for i in candidates]), spare
        for i in candidates:
            more = min(bound - counts[i], max(1, budget * loads[i] // mass), spare)
            counts[i] = counts[i] + more
            spare = spare - more
    return np.array([bound] + counts)


def uneven(key, count, total, limit, skew):
    if count == 2:
        one = jax.random.randint(key, (), max(1, total - limit), min(limit, total - 1) + 1)
        return jnp.stack([one, total - one])
    sizes = jnp.asarray(split_up(count, total, limit, skew), jnp.int32)
    twos = (count - 1) // 2
    source_of, taker = sizes[1:1 + 2 * twos:2], sizes[2:2 + 2 * twos:2]
    margin = jnp.minimum(source_of - 1, limit - taker)
    shifted = jax.random.randint(jax.random.fold_in(key, 1), (twos,), 0, 1 << 20) % (margin + 1)
    sizes = sizes.at[1:1 + 2 * twos:2].set(source_of - shifted).at[2:2 + 2 * twos:2].set(taker + shifted)
    return sizes[jax.random.permutation(jax.random.fold_in(key, 2), count)]


def gaussian(own_key, dims, spread, limit, shards=(), held_as=jnp.bfloat16):
    result = jax.random.normal(own_key, dims, jnp.float32) * spread
    if len(shards) > 0:
        result = block_levels(own_key, dims, shards, -0.22, 0.18) * result
    return jnp.clip(result, min=-limit, max=limit).astype(held_as)


def gaussian_with(stream_key, shape, deviation, limit, cuts, heavy, kind=jnp.bfloat16):
    array = deviation * jax.random.normal(stream_key, shape, jnp.float32)
    if cuts:
        array = array * block_levels(stream_key, shape, cuts, -0.22, 0.18)
    return jnp.clip(strengthened(array, jax.random.fold_in(stream_key, 3), *heavy), -limit, limit).astype(kind)


def setup_inputs(seed: int = 0) -> dict:
    arg_keys = jax.random.split(jax.random.key(seed), 16)
    return {
        "layer_input": gaussian_with(arg_keys[0], (TOKENS, D), 1.0, 6.0, ((0, 32),), (0, 1, 32, 2.75), jnp.float32),
        "cotangent": gaussian(arg_keys[1], (TOKENS, D), 1.0, 6.0, ((0, 32),), jnp.float32),
        "seq_lengths": uneven(arg_keys[2], SEQS, TOKENS, MOST, 2).astype(jnp.int32),
        "gain_attn": jnp.clip(1.0 + 0.1 * jax.random.normal(arg_keys[3], (D,), jnp.float32), 0.5, 1.5).astype(jnp.bfloat16),
        "beta_attn": gaussian(arg_keys[4], (D,), 0.5, 3.0, ((0, 8),)),
        "gain_mlp": jnp.clip(1.0 + 0.1 * jax.random.normal(arg_keys[5], (D,), jnp.float32), 0.5, 1.5).astype(jnp.bfloat16),
        "beta_mlp": gaussian(arg_keys[6], (D,), 0.5, 3.0, ((0, 8),)),
        "qkv_weight": gaussian(arg_keys[7], (D, 3, H, HD), D ** -0.5, 0.21875, ((0, 8),)),
        "qkv_bias": gaussian(arg_keys[8], (3 * D,), 0.5, 3.0, ((0, 8),)),
        "dense_weight": gaussian(arg_keys[9], (D, D), (D // 16) ** -0.5, 0.875, ((1, 8),)),
        "dense_bias": gaussian(arg_keys[10], (D,), 0.5, 3.0, ((0, 8),)),
        "up_weight": gaussian(arg_keys[11], (D, FF), D ** -0.5, 0.21875, ((0, 8), (1, 4))),
        "up_bias": gaussian(arg_keys[12], (FF,), 0.5, 3.0, ((0, 8),)),
        "down_weight": gaussian(arg_keys[13], (D, FF), (FF // 2) ** -0.5, 0.15625, ((0, 8), (1, 4))),
        "down_bias": gaussian(arg_keys[14], (D,), 0.5, 3.0, ((0, 8),)),
    }


EPS = 1e-05
NEG_FILL = -1e+30

def norm_parts(inputs):
    row_mean = lax.optimization_barrier(jnp.mean(inputs, axis=-1, keepdims=True))
    centred = inputs - row_mean
    row_var = lax.optimization_barrier(jnp.mean(centred * centred, axis=-1, keepdims=True))
    inv_std = lax.rsqrt(row_var + EPS)
    return (centred * inv_std, inv_std)

def norm_back(grad_hat, normed, inv_std):
    first_mean = lax.optimization_barrier(jnp.mean(grad_hat, axis=-1, keepdims=True))
    second_mean = lax.optimization_barrier(jnp.mean(grad_hat * normed, axis=-1, keepdims=True))
    return inv_std * (grad_hat - first_mean - normed * second_mean)

def gelu_value(pre_act):
    return 0.5 * pre_act * (1.0 + lax.erf(pre_act * (1.0 / math.sqrt(2.0))))

def gelu_slope(pre_act):
    cumulative = 0.5 * (1.0 + lax.erf(pre_act * (1.0 / math.sqrt(2.0))))
    return cumulative + pre_act * jnp.exp(-0.5 * pre_act * pre_act) * (1.0 / math.sqrt(2.0 * math.pi))

def rotary_tables(positions):
    half_rot = ROT // 2
    inverse = jnp.exp(jnp.arange(half_rot, dtype=jnp.float32) * (-2.0 * math.log(10000.0) / ROT))
    phase_angle = positions.astype(jnp.float32)[:, None] * inverse[None, :]
    return (jnp.cos(phase_angle)[:, None, :], jnp.sin(phase_angle)[:, None, :])

def rotate(vectors, cosine, sine_table):
    half_rot = ROT // 2
    first_half = vectors[..., :half_rot]
    second_half = vectors[..., half_rot:ROT]
    return jnp.concatenate([first_half * cosine - second_half * sine_table, second_half * cosine + first_half * sine_table, vectors[..., ROT:]], axis=-1)

def rotate_back(grads, cosine, sine_table):
    half_rot = ROT // 2
    first_half = grads[..., :half_rot]
    second_half = grads[..., half_rot:ROT]
    return jnp.concatenate([first_half * cosine + second_half * sine_table, second_half * cosine - first_half * sine_table, grads[..., ROT:]], axis=-1)

def token_segments(seq_lengths, token_index):
    seq_ends = jnp.cumsum(seq_lengths, dtype=jnp.int32)
    seq_starts = seq_ends - seq_lengths
    segment_ids = lax.optimization_barrier(jnp.sum((seq_ends[None, :] <= token_index[:, None]).astype(jnp.int32), axis=1, dtype=jnp.int32))
    chosen = segment_ids[:, None] == jnp.arange(seq_lengths.shape[0], dtype=jnp.int32)[None, :]
    first_token = lax.optimization_barrier(jnp.sum(jnp.where(chosen, seq_starts[None, :], 0), axis=1, dtype=jnp.int32))
    return (segment_ids, token_index - first_token)

def rounded(values):
    return lax.optimization_barrier(values.astype(jnp.bfloat16)).astype(jnp.float32)

def reference(layer_input, cotangent, seq_lengths, gain_attn, beta_attn, gain_mlp, beta_mlp, qkv_weight, qkv_bias, dense_weight, dense_bias, up_weight, up_bias, down_weight, down_bias):
    token_total = layer_input.shape[0]
    score_scale = 1.0 / math.sqrt(HD)
    normed, inv_std = norm_parts(layer_input)
    h_attn = (normed * gain_attn.astype(jnp.float32) + beta_attn.astype(jnp.float32)).astype(jnp.bfloat16)
    h_mlp = (normed * gain_mlp.astype(jnp.float32) + beta_mlp.astype(jnp.float32)).astype(jnp.bfloat16)
    token_index = jnp.arange(token_total, dtype=jnp.int32)
    segment_ids, positions = token_segments(seq_lengths, token_index)
    cosine, sine_table = rotary_tables(positions)
    w_qkv = qkv_weight.reshape(D, 3 * D)
    projected = jnp.dot(h_attn, w_qkv, preferred_element_type=jnp.float32) + qkv_bias.astype(jnp.float32)[None, :]
    projected = projected.reshape(token_total, 3, H, HD)
    queries = rotate(projected[:, 0], cosine, sine_table).astype(jnp.bfloat16)
    key_rows = rotate(projected[:, 1], cosine, sine_table).astype(jnp.bfloat16)
    value_rows = projected[:, 2].astype(jnp.bfloat16)
    block_rows = min(512, token_total)
    block_count = token_total // block_rows
    key_reach = MOST
    window = key_reach + block_rows
    padded_keys = jnp.pad(key_rows, ((key_reach, 0), (0, 0), (0, 0)))
    padded_values = jnp.pad(value_rows, ((key_reach, 0), (0, 0), (0, 0)))
    padded_segments = jnp.pad(segment_ids, (key_reach, 0), constant_values=-1)
    causal = jnp.arange(window, dtype=jnp.int32)[None, :] <= key_reach + jnp.arange(block_rows, dtype=jnp.int32)[:, None]

    def block_setup(query_start):
        query_block = lax.dynamic_slice_in_dim(queries, query_start, block_rows, 0).astype(jnp.float32)
        key_block = lax.dynamic_slice_in_dim(padded_keys, query_start, window, 0).astype(jnp.float32)
        value_block = lax.dynamic_slice_in_dim(padded_values, query_start, window, 0).astype(jnp.float32)
        query_segs = lax.dynamic_slice_in_dim(segment_ids, query_start, block_rows, 0)
        key_segs = lax.dynamic_slice_in_dim(padded_segments, query_start, window, 0)
        key_mask = ((query_segs[:, None] == key_segs[None, :]) & causal)[None]
        scores = jnp.einsum('qhd,khd->hqk', query_block, key_block) * score_scale
        return (query_block, key_block, value_block, key_mask, scores)

    def forward_block(query_start):
        query_block, key_block, value_block, key_mask, scores = block_setup(query_start)
        masked = jnp.where(key_mask, scores, NEG_FILL)
        row_top = lax.optimization_barrier(jnp.max(masked, axis=-1, keepdims=True))
        row_total = lax.optimization_barrier(jnp.sum(jnp.where(key_mask, jnp.exp(masked - row_top), 0.0), axis=-1, keepdims=True))
        row_lse = row_top + jnp.log(row_total)
        attn_probs = jnp.where(key_mask, jnp.exp(masked - row_lse), 0.0)
        mixed = jnp.einsum('hqk,khd->qhd', rounded(attn_probs), value_block)
        return (mixed.astype(jnp.bfloat16), row_lse[..., 0])
    block_starts = jnp.arange(block_count, dtype=jnp.int32) * block_rows
    mixed_blocks, lse_blocks = lax.map(forward_block, block_starts)
    attn_heads = mixed_blocks.reshape(token_total, H, HD)
    attn_flat = attn_heads.reshape(token_total, D)
    attn_out = jnp.dot(attn_flat, dense_weight, preferred_element_type=jnp.float32) + dense_bias.astype(jnp.float32)[None, :]
    pre_act = jnp.dot(h_mlp, up_weight, preferred_element_type=jnp.float32) + up_bias.astype(jnp.float32)[None, :]
    activation = gelu_value(pre_act).astype(jnp.bfloat16)
    mlp_out = jnp.dot(activation, down_weight.T, preferred_element_type=jnp.float32) + down_bias.astype(jnp.float32)[None, :]
    layer_output = layer_input + attn_out + mlp_out
    grad_low = cotangent.astype(jnp.bfloat16)
    grad_dense_weight = jnp.dot(attn_flat.T, grad_low, preferred_element_type=jnp.float32)
    bias_grad = lax.optimization_barrier(jnp.sum(cotangent, axis=0))
    head_grads = jnp.dot(grad_low, dense_weight.T, preferred_element_type=jnp.float32).astype(jnp.bfloat16).reshape(token_total, H, HD)
    row_delta = lax.optimization_barrier(jnp.sum(head_grads.astype(jnp.float32) * attn_heads.astype(jnp.float32), axis=-1))

    def backward_block(carried, block_number):
        key_acc, value_acc = carried
        query_start = block_number * block_rows
        query_block, key_block, value_block, key_mask, scores = block_setup(query_start)
        row_lse = lse_blocks[block_number]
        attn_probs = jnp.where(key_mask, jnp.exp(scores - row_lse[..., None]), 0.0)
        out_grads = lax.dynamic_slice_in_dim(head_grads, query_start, block_rows, 0).astype(jnp.float32)
        delta_block = lax.dynamic_slice_in_dim(row_delta, query_start, block_rows, 0).T
        prob_grads = jnp.einsum('qhd,khd->hqk', out_grads, value_block)
        score_grads = rounded(attn_probs * (prob_grads - delta_block[..., None]) * score_scale)
        query_grads = jnp.einsum('hqk,khd->qhd', score_grads, key_block)
        key_part = jnp.einsum('hqk,qhd->khd', score_grads, query_block)
        value_part = jnp.einsum('hqk,qhd->khd', rounded(attn_probs), out_grads)
        key_acc = lax.dynamic_update_slice_in_dim(key_acc, lax.dynamic_slice_in_dim(key_acc, query_start, window, 0) + key_part, query_start, 0)
        value_acc = lax.dynamic_update_slice_in_dim(value_acc, lax.dynamic_slice_in_dim(value_acc, query_start, window, 0) + value_part, query_start, 0)
        return ((key_acc, value_acc), query_grads)
    empty_acc = jnp.zeros((token_total + key_reach, H, HD), jnp.float32)
    (key_acc, value_acc), query_blocks = lax.scan(backward_block, (empty_acc, empty_acc), jnp.arange(block_count, dtype=jnp.int32))
    query_grads = query_blocks.reshape(token_total, H, HD)
    key_grads = key_acc[key_reach:]
    value_grads = value_acc[key_reach:]
    qkv_grads = jnp.stack([rotate_back(query_grads, cosine, sine_table), rotate_back(key_grads, cosine, sine_table), value_grads], axis=1)
    qkv_grads = qkv_grads.astype(jnp.bfloat16).reshape(token_total, 3 * D)
    grad_qkv_weight = jnp.dot(h_attn.T, qkv_grads, preferred_element_type=jnp.float32).reshape(D, 3, H, HD)
    grad_qkv_bias = lax.optimization_barrier(jnp.sum(qkv_grads.astype(jnp.float32), axis=0))
    attn_input_grad = jnp.dot(qkv_grads, w_qkv.T, preferred_element_type=jnp.float32)
    hidden_grads = jnp.dot(grad_low, down_weight, preferred_element_type=jnp.float32) * gelu_slope(pre_act)
    hidden_low = hidden_grads.astype(jnp.bfloat16)
    grad_down_weight = jnp.dot(grad_low.T, activation, preferred_element_type=jnp.float32)
    grad_up_weight = jnp.dot(h_mlp.T, hidden_low, preferred_element_type=jnp.float32)
    grad_up_bias = lax.optimization_barrier(jnp.sum(hidden_grads, axis=0))
    mlp_input_grad = jnp.dot(hidden_low, up_weight.T, preferred_element_type=jnp.float32)
    grad_gain_attn = lax.optimization_barrier(jnp.sum(attn_input_grad * normed, axis=0))
    grad_beta_attn = lax.optimization_barrier(jnp.sum(attn_input_grad, axis=0))
    grad_gain_mlp = lax.optimization_barrier(jnp.sum(mlp_input_grad * normed, axis=0))
    grad_beta_mlp = lax.optimization_barrier(jnp.sum(mlp_input_grad, axis=0))
    grad_hat = attn_input_grad * gain_attn.astype(jnp.float32) + mlp_input_grad * gain_mlp.astype(jnp.float32)
    input_grad = cotangent + norm_back(grad_hat, normed, inv_std)
    return (layer_output, input_grad, grad_qkv_weight, grad_qkv_bias, grad_dense_weight, bias_grad, grad_gain_attn, grad_beta_attn, grad_gain_mlp, grad_beta_mlp, grad_up_weight, grad_up_bias, grad_down_weight, bias_grad)
```

```python
import functools
import math

import jax
import jax.numpy as jnp
from jax import lax
from jax.experimental import pallas as pl
from jax.experimental.pallas import tpu as pltpu
from jax.sharding import PartitionSpec as P

ROT = 16
SPAN = 16


EPS = 1e-05
NEG_FILL = -1e30


def norm_parts(inputs):
    row_mean = jnp.mean(inputs, axis=-1, keepdims=True)
    centred = inputs - row_mean
    row_var = jnp.mean(centred * centred, axis=-1, keepdims=True)
    inv_std = lax.rsqrt(row_var + EPS)
    return (centred * inv_std, inv_std)


def norm_back(grad_hat, normed, inv_std):
    first_mean = jnp.mean(grad_hat, axis=-1, keepdims=True)
    second_mean = jnp.mean(grad_hat * normed, axis=-1, keepdims=True)
    return inv_std * (grad_hat - first_mean - normed * second_mean)


def gelu_value(pre_act):
    return 0.5 * pre_act * (1.0 + lax.erf(pre_act * (1.0 / math.sqrt(2.0))))


def gelu_slope(pre_act):
    cumulative = 0.5 * (1.0 + lax.erf(pre_act * (1.0 / math.sqrt(2.0))))
    return cumulative + pre_act * jnp.exp(-0.5 * pre_act * pre_act) * (
        1.0 / math.sqrt(2.0 * math.pi)
    )


def rotary_tables(positions):
    half_rot = ROT // 2
    inverse = jnp.exp(jnp.arange(half_rot, dtype=jnp.float32) * (-2.0 * math.log(10000.0) / ROT))
    phase_angle = positions.astype(jnp.float32)[:, None] * inverse[None, :]
    return (jnp.cos(phase_angle)[:, None, :], jnp.sin(phase_angle)[:, None, :])


def rotate(vectors, cosine, sine_table):
    half_rot = ROT // 2
    first_half = vectors[..., :half_rot]
    second_half = vectors[..., half_rot:ROT]
    return jnp.concatenate(
        [
            first_half * cosine - second_half * sine_table,
            second_half * cosine + first_half * sine_table,
            vectors[..., ROT:],
        ],
        axis=-1,
    )


def rotate_back(grads, cosine, sine_table):
    half_rot = ROT // 2
    first_half = grads[..., :half_rot]
    second_half = grads[..., half_rot:ROT]
    return jnp.concatenate(
        [
            first_half * cosine + second_half * sine_table,
            second_half * cosine - first_half * sine_table,
            grads[..., ROT:],
        ],
        axis=-1,
    )


def token_segments(seq_lengths, token_index):
    seq_ends = jnp.cumsum(seq_lengths, dtype=jnp.int32)
    seq_starts = seq_ends - seq_lengths
    segment_ids = jnp.sum(
        (seq_ends[None, :] <= token_index[:, None]).astype(jnp.int32), axis=1, dtype=jnp.int32
    )
    chosen = segment_ids[:, None] == jnp.arange(seq_lengths.shape[0], dtype=jnp.int32)[None, :]
    first_token = jnp.sum(jnp.where(chosen, seq_starts[None, :], 0), axis=1, dtype=jnp.int32)
    return (segment_ids, token_index - first_token)


def contract_rows(left, right):
    return lax.dot_general(
        left, right, (((0,), (0,)), ((), ())), preferred_element_type=jnp.float32
    )


def contract_cols(left, right):
    return lax.dot_general(
        left, right, (((1,), (1,)), ((), ())), preferred_element_type=jnp.float32
    )


def place():
    rank = lax.axis_index("fsdp")
    return rank // 2, rank % 2, lax.axis_index("mp")


def enter(chip_count, model_count):
    chip, core, model = place()
    barrier = pltpu.get_barrier_semaphore()
    peers = []
    if chip_count:
        peers.append((chip * 2 + (1 - core), model))
        for step in range(1, chip_count):
            peers.append((((chip + step) % chip_count) * 2 + core, model))
    for step in range(1, model_count):
        peers.append((chip * 2 + core, (model + step) % model_count))
    for peer in peers:
        pl.semaphore_signal(
            barrier, inc=1, device_id=peer, device_id_type=pl.DeviceIdType.MESH
        )
    pl.semaphore_wait(barrier, len(peers))


class Copies:
    def __init__(self, send, recv, local):
        self.send, self.recv, self.local = send, recv, local
        self.used, self.used_local = 0, 0

    def remote(self, source, target, peer):
        index = self.used
        self.used += 1
        return pltpu.make_async_remote_copy(
            src_ref=source,
            dst_ref=target,
            send_sem=self.send.at[index],
            recv_sem=self.recv.at[index],
            device_id=peer,
            device_id_type=pl.DeviceIdType.MESH,
        )

    def within(self, source, target):
        index = self.used_local
        self.used_local += 1
        return pltpu.make_async_copy(source, target, self.local.at[index])


def model_exchange(copies, source, target, model_count, gather):
    chip, core, model = place()
    started = []
    own = copies.within(source if gather else source.at[model], target.at[model])
    own.start()
    for step in range(1, model_count):
        peer = (model + step) % model_count
        copy = copies.remote(
            source if gather else source.at[peer], target.at[model], (chip * 2 + core, peer)
        )
        copy.start()
        started.append(copy)
    return [own] + started


def gather_start(copies, source, target, chip_count):
    chip, core, model = place()
    rank = chip * 2 + core
    own = copies.within(source, target.at[rank])
    own.start()
    to_pair = copies.remote(source, target.at[rank], (chip * 2 + (1 - core), model))
    to_pair.start()
    far = []
    for step in range(1, chip_count):
        peer = ((chip + step) % chip_count) * 2 + core
        copy = copies.remote(source, target.at[rank], (peer, model))
        copy.start()
        far.append(copy)
    return [own, to_pair], far


def gather_forward(copies, target, far, chip_count):
    chip, core, model = place()
    waits = []
    for step in range(1, chip_count):
        far[step - 1].wait_recv()
        slot = ((chip + chip_count - step) % chip_count) * 2 + core
        copy = copies.remote(target.at[slot], target.at[slot], (chip * 2 + (1 - core), model))
        copy.start()
        waits.append(copy)
    return waits


def open_kernel(chip_count, model_count, w_ref, v_ref, t_ref, w_out, v_out, t_out, s, r, l):
    enter(chip_count, model_count)
    copies = Copies(s, r, l)
    tokens = model_exchange(copies, t_ref, t_out, model_count, True)
    near_v, far_v = gather_start(copies, v_ref, v_out, chip_count)
    near_w, far_w = gather_start(copies, w_ref, w_out, chip_count)
    more = gather_forward(copies, v_out, far_v, chip_count)
    more += gather_forward(copies, w_out, far_w, chip_count)
    for copy in far_v + far_w:
        copy.wait_send()
    for copy in tokens + near_v + near_w + more:
        copy.wait()


def keys_kernel(chip_count, hops, x_ref, out, s, r, l):
    enter(chip_count, 1)
    copies = Copies(s, r, l)
    chip, core, model = place()
    pair = (chip * 2 + (1 - core), model)
    near = copies.remote(x_ref, out.at[0, core], pair)
    near.start()
    far, onward = [], []
    for step in range(1, hops + 1):
        target = ((chip + step) % chip_count) * 2 + core
        far.append(copies.remote(x_ref, out.at[step, core], (target, model)))
        onward.append(copies.remote(out.at[step, core], out.at[step, core], pair))

        @pl.when(chip + step < chip_count)
        def _(copy=far[-1]):
            copy.start()

    for step in range(1, hops + 1):

        @pl.when(chip >= step)
        def _(arrived=far[step - 1], copy=onward[step - 1]):
            arrived.wait_recv()
            copy.start()

    near.wait()
    for step in range(1, hops + 1):

        @pl.when(chip >= step)
        def _(copy=onward[step - 1]):
            copy.wait()

        @pl.when(chip + step < chip_count)
        def _(copy=far[step - 1]):
            copy.wait_send()


def pair_kernel(
    chip_count, model_count, hops, p_ref, b_ref, out, b_out, near_buf, sums, far_buf, s, r, l
):
    enter(chip_count, model_count)
    copies = Copies(s, r, l)
    chip, core, model = place()
    pair = (chip * 2 + (1 - core), model)
    near = [
        copies.remote(p_ref.at[1 - core, step], near_buf.at[step], pair)
        for step in range(hops + 1)
    ]
    for copy in near:
        copy.start()
    branch = model_exchange(copies, b_ref, b_out, model_count, False)
    far = []
    for step in list(range(1, hops + 1)) + [0]:
        near[step].wait_recv()
        total = p_ref[core, step].astype(jnp.float32) + near_buf[step].astype(jnp.float32)
        if step == 0:
            out[...] = total
            continue
        sums[step - 1] = total.astype(sums.dtype)
        target = ((chip + chip_count - step) % chip_count) * 2 + core
        far.append(copies.remote(sums.at[step - 1], far_buf.at[step - 1], (target, model)))

        @pl.when(chip >= step)
        def _(copy=far[-1]):
            copy.start()

    for step in range(1, hops + 1):

        @pl.when(chip + step < chip_count)
        def _(copy=far[step - 1], step=step):
            copy.wait_recv()
            out[...] += far_buf[step - 1].astype(jnp.float32)

    for step in range(1, hops + 1):

        @pl.when(chip >= step)
        def _(copy=far[step - 1]):
            copy.wait_send()

    for copy in near:
        copy.wait_send()
    for copy in branch:
        copy.wait()


def reduce_near(copies, source, near_buf, chip_count):
    chip, core, model = place()
    near = []
    for step in list(range(1, chip_count)) + [0]:
        target = (chip + step) % chip_count
        copy = copies.remote(
            source.at[target, 1 - core], near_buf.at[step], (chip * 2 + (1 - core), model)
        )
        copy.start()
        near.append(copy)
    return near


def reduce_far(copies, source, near_buf, sums, far_buf, out, near, chip_count):
    chip, core, model = place()
    far = []
    for index, step in enumerate(list(range(1, chip_count)) + [0]):
        target = (chip + step) % chip_count
        near[index].wait_recv()
        total = source[target, core].astype(jnp.float32) + near_buf[step].astype(jnp.float32)
        if step == 0:
            out[...] = total
            continue
        sums[step - 1] = total.astype(sums.dtype)
        copy = copies.remote(sums.at[step - 1], far_buf.at[step - 1], (target * 2 + core, model))
        copy.start()
        far.append(copy)
    return far


def reduce_end(out, far_buf, near, far):
    for index, copy in enumerate(far):
        copy.wait_recv()
        out[...] += far_buf[index].astype(jnp.float32)
    for copy in near + far:
        copy.wait_send()


def close_kernel(
    chip_count, model_count, g_ref, v_ref, b_ref, g_out, v_out, b_out,
    g_near, g_sums, g_far, v_near, v_sums, v_far, s, r, l,
):
    enter(chip_count, model_count)
    copies = Copies(s, r, l)
    v_started = reduce_near(copies, v_ref, v_near, chip_count)
    g_started = reduce_near(copies, g_ref, g_near, chip_count)
    branch = model_exchange(copies, b_ref, b_out, model_count, False)
    v_sent = reduce_far(copies, v_ref, v_near, v_sums, v_far, v_out, v_started, chip_count)
    g_sent = reduce_far(copies, g_ref, g_near, g_sums, g_far, g_out, g_started, chip_count)
    reduce_end(v_out, v_far, v_started, v_sent)
    reduce_end(g_out, g_far, g_started, g_sent)
    for copy in branch:
        copy.wait()


def last_kernel(model_count, g_ref, v_ref, g_out, v_out, s, r, l):
    enter(0, model_count)
    copies = Copies(s, r, l)
    started = model_exchange(copies, v_ref, v_out, model_count, True)
    started += model_exchange(copies, g_ref, g_out, model_count, True)
    for copy in started:
        copy.wait()


def call(kernel, number, operands, outs, spaces, out_spaces, scratch, remote, local):
    return pl.pallas_call(
        kernel,
        out_shape=[jax.ShapeDtypeStruct(shape, dtype) for shape, dtype in outs],
        in_specs=[pl.BlockSpec(memory_space=space) for space in spaces],
        out_specs=[pl.BlockSpec(memory_space=space) for space in out_spaces],
        scratch_shapes=scratch
        + [
            pltpu.SemaphoreType.DMA((remote,)),
            pltpu.SemaphoreType.DMA((remote,)),
            pltpu.SemaphoreType.DMA((max(local, 1),)),
        ],
        compiler_params=pltpu.CompilerParams(collective_id=number, has_side_effects=True),
    )(*operands)


def on_device(
    layer_input,
    cotangent,
    seq_lengths,
    gain_attn,
    beta_attn,
    gain_mlp,
    beta_mlp,
    qkv_weight,
    qkv_bias,
    dense_weight,
    dense_bias,
    up_weight,
    up_bias,
    down_weight,
    down_bias,
):
    fsdp_count = lax.axis_size("fsdp")
    model_count = lax.axis_size("mp")
    chip_count = fsdp_count // 2
    fsdp_rank = lax.axis_index("fsdp")
    model_rank = lax.axis_index("mp")
    chip, core = fsdp_rank // 2, fsdp_rank % 2
    tok_dev, model_width = layer_input.shape
    owned = qkv_weight.shape[0]
    head_count, head_dim = qkv_weight.shape[2:]
    local_heads = head_count // model_count
    local_width = local_heads * head_dim
    hidden_local = up_weight.shape[1]
    hidden_total = hidden_local * model_count
    group_rows = model_count * tok_dev
    key_reach = min(SPAN * group_rows, group_rows * fsdp_count // 2)
    hops = (key_reach // group_rows + 1) // 2
    score_scale = 1.0 / math.sqrt(head_dim)
    bf16, f32 = jnp.bfloat16, jnp.float32
    vmem, anywhere = pltpu.VMEM, pl.ANY

    own_qkv = lax.dynamic_slice_in_dim(qkv_weight, model_rank * local_heads, local_heads, 2)
    own_dense = lax.dynamic_slice_in_dim(dense_weight, model_rank * local_width, local_width, 0)
    pack = jnp.concatenate(
        [own_qkv.reshape(owned, 3 * local_width), own_dense.T, up_weight, down_weight], axis=1
    )
    vectors = (qkv_bias, dense_bias, up_bias, down_bias, gain_attn, beta_attn, gain_mlp, beta_mlp)
    vector_pack = jnp.concatenate(vectors).astype(f32)[None, :]
    normed, inv_std = norm_parts(layer_input)
    grad_low = cotangent.astype(bf16)
    token_pack = jnp.concatenate([normed.astype(bf16), grad_low], axis=1)
    columns = pack.shape[1]
    weights, vector_all, token_rows = call(
        functools.partial(open_kernel, chip_count, model_count),
        0,
        (pack, vector_pack, token_pack),
        [
            ((fsdp_count,) + pack.shape, bf16),
            ((fsdp_count,) + vector_pack.shape, f32),
            ((model_count,) + token_pack.shape, bf16),
        ],
        [anywhere] * 3,
        [anywhere] * 3,
        [],
        (model_count - 1) + 2 * (2 * chip_count - 1),
        3,
    )
    weights = weights.reshape(model_width, columns)
    w_qkv = weights[:, : 3 * local_width]
    w_dense = weights[:, 3 * local_width : 4 * local_width]
    w_up = weights[:, 4 * local_width : 4 * local_width + hidden_local]
    w_down = weights[:, 4 * local_width + hidden_local :]
    full = []
    at = 0
    for vector in vectors:
        full.append(vector_all[:, 0, at : at + vector.shape[0]].reshape(-1))
        at += vector.shape[0]
    full_qkv_bias, full_dense_bias, full_up_bias, full_down_bias = full[:4]
    gain_one, shift_one, gain_two, shift_two = full[4:]
    local_qkv_bias = lax.dynamic_slice_in_dim(
        full_qkv_bias.reshape(3, head_count, head_dim), model_rank * local_heads, local_heads, 1
    ).reshape(3 * local_width)
    local_up_bias = lax.dynamic_slice_in_dim(
        full_up_bias, model_rank * hidden_local, hidden_local, 0
    )
    token_rows = token_rows.reshape(group_rows, 2 * model_width)
    normed_rows = token_rows[:, :model_width].astype(f32)
    grad_rows = token_rows[:, model_width:]
    h_attn = (normed_rows * gain_one + shift_one).astype(bf16)
    h_mlp = (normed_rows * gain_two + shift_two).astype(bf16)

    group_index = fsdp_rank * group_rows + jnp.arange(group_rows, dtype=jnp.int32)
    group_seg, group_pos = token_segments(seq_lengths, group_index)
    group_cos, group_sin = rotary_tables(group_pos)
    causal_mask = (
        jnp.arange(group_rows, dtype=jnp.int32)[None, :]
        <= jnp.arange(group_rows, dtype=jnp.int32)[:, None]
    )
    projected = jnp.dot(h_attn, w_qkv, preferred_element_type=f32) + local_qkv_bias[None, :]
    projected = projected.reshape(group_rows, 3, local_heads, head_dim)
    query_rows = rotate(projected[:, 0], group_cos, group_sin).astype(bf16)
    own_keys = rotate(projected[:, 1], group_cos, group_sin).astype(bf16)
    own_pair = jnp.concatenate(
        [own_keys.reshape(group_rows, local_width),
         projected[:, 2].astype(bf16).reshape(group_rows, local_width)], axis=1
    )
    (others,) = call(
        functools.partial(keys_kernel, chip_count, hops),
        1,
        (own_pair,),
        [((hops + 1, 2) + own_pair.shape, bf16)],
        [anywhere],
        [anywhere],
        [],
        1 + 2 * hops,
        0,
    )

    pre_act = jnp.dot(h_mlp, w_up, preferred_element_type=f32) + local_up_bias[None, :]
    activation = gelu_value(pre_act).astype(bf16)
    mlp_part = contract_cols(activation, w_down)
    hidden_grads = jnp.dot(grad_rows, w_down, preferred_element_type=f32) * gelu_slope(pre_act)
    hidden_low = hidden_grads.astype(bf16)
    mlp_input_part = contract_cols(hidden_low, w_up)

    key_sets = [(own_pair, group_seg, True, None)]
    for step in range(hops + 1):
        for side in range(2):
            source = (chip - step) * 2 + side
            if step == 0:
                if side == 1:
                    continue
                valid = core == 1
            else:
                valid = source >= 0
            pair = others[step, side]
            earlier = source * group_rows + jnp.arange(group_rows, dtype=jnp.int32)
            earlier_seg, unused = token_segments(seq_lengths, earlier)
            earlier_seg = jnp.where(valid, earlier_seg, -1)
            key_sets.append((pair, earlier_seg, False, (step, side)))

    def is_live(key_segs):
        return key_segs[-1] == group_seg[0]

    def block_scores(pair, key_segs, causal):
        key_block = pair[:, :local_width].reshape(group_rows, local_heads, head_dim)
        scores = (
            jnp.einsum("qhd,khd->hqk", query_rows, key_block, preferred_element_type=f32)
            * score_scale
        )
        key_mask = group_seg[:, None] == key_segs[None, :]
        if causal:
            key_mask = key_mask & causal_mask
        return (scores, key_mask[None])

    def stats_update(carried_state, pair, key_segs):
        row_top, row_total = carried_state
        scores, key_mask = block_scores(pair, key_segs, False)
        masked = jnp.where(key_mask, scores, NEG_FILL)
        new_top = jnp.maximum(row_top, jnp.max(masked, axis=-1))
        new_total = row_total * jnp.exp(row_top - new_top) + jnp.sum(
            jnp.where(key_mask, jnp.exp(masked - new_top[..., None]), 0.0), axis=-1
        )
        return (new_top, new_total)

    scores, key_mask = block_scores(own_pair, group_seg, True)
    masked = jnp.where(key_mask, scores, NEG_FILL)
    row_top = jnp.max(masked, axis=-1)
    row_total = jnp.sum(jnp.where(key_mask, jnp.exp(masked - row_top[..., None]), 0.0), axis=-1)
    for pair, key_segs, causal, slot in key_sets[1:]:
        row_top, row_total = lax.cond(
            is_live(key_segs),
            lambda carried_state: stats_update(carried_state, pair, key_segs),
            lambda carried_state: carried_state,
            (row_top, row_total),
        )
    row_lse = row_top + jnp.log(row_total)

    def block_output(pair, key_segs, causal):
        scores, key_mask = block_scores(pair, key_segs, causal)
        attn_probs = jnp.where(key_mask, jnp.exp(scores - row_lse[..., None]), 0.0).astype(bf16)
        value_block = pair[:, local_width:].reshape(group_rows, local_heads, head_dim)
        return jnp.einsum("hqk,khd->qhd", attn_probs, value_block, preferred_element_type=f32)

    zero_heads = jnp.zeros((group_rows, local_heads, head_dim), f32)
    mixed = block_output(own_pair, group_seg, True)
    for pair, key_segs, causal, slot in key_sets[1:]:
        mixed = mixed + lax.cond(
            is_live(key_segs), lambda: block_output(pair, key_segs, False), lambda: zero_heads
        )
    out_heads = mixed.astype(bf16)
    out_flat = out_heads.reshape(group_rows, local_width)
    branch_part = (mlp_part + contract_cols(out_flat, w_dense)).astype(bf16)
    head_grads = (
        jnp.dot(grad_rows, w_dense, preferred_element_type=f32)
        .astype(bf16)
        .reshape(group_rows, local_heads, head_dim)
    )
    row_delta = jnp.sum(head_grads.astype(f32) * out_heads.astype(f32), axis=-1).T

    def block_grads(pair, key_segs, causal):
        scores, key_mask = block_scores(pair, key_segs, causal)
        attn_probs = jnp.where(key_mask, jnp.exp(scores - row_lse[..., None]), 0.0)
        key_block = pair[:, :local_width].reshape(group_rows, local_heads, head_dim)
        value_block = pair[:, local_width:].reshape(group_rows, local_heads, head_dim)
        prob_grads = jnp.einsum(
            "qhd,khd->hqk", head_grads, value_block, preferred_element_type=f32
        )
        score_grads = (attn_probs * (prob_grads - row_delta[..., None]) * score_scale).astype(bf16)
        query_grads = jnp.einsum(
            "hqk,khd->qhd", score_grads, key_block, preferred_element_type=f32
        )
        key_part = jnp.einsum(
            "hqk,qhd->khd", score_grads, query_rows, preferred_element_type=f32
        )
        value_part = jnp.einsum(
            "hqk,qhd->khd", attn_probs.astype(bf16), head_grads, preferred_element_type=f32
        )
        return (
            query_grads,
            jnp.concatenate(
                [
                    key_part.reshape(group_rows, local_width),
                    value_part.reshape(group_rows, local_width),
                ],
                axis=1,
            ).astype(bf16),
        )

    zero_pair = jnp.zeros((group_rows, 2 * local_width), bf16)
    query_grads, own_part = block_grads(own_pair, group_seg, True)
    parts = {}
    for pair, key_segs, causal, slot in key_sets[1:]:
        query_part, parts[slot] = lax.cond(
            is_live(key_segs),
            lambda: block_grads(pair, key_segs, False),
            lambda: (zero_heads, zero_pair),
        )
        query_grads = query_grads + query_part
    pair_part = parts[(0, 0)]
    first = core == 0
    near_parts = [jnp.where(first, own_part, pair_part), jnp.where(first, zero_pair, own_part)]
    part_stack = jnp.stack(
        [
            jnp.stack([near_parts[side]] + [parts[(step, side)] for step in range(1, hops + 1)])
            for side in range(2)
        ]
    )
    branch_stack = branch_part.reshape(model_count, tok_dev, model_width)
    block_shape = own_pair.shape
    pair_grads, branch_rows = call(
        functools.partial(pair_kernel, chip_count, model_count, hops),
        2,
        (part_stack, branch_stack),
        [(block_shape, f32), (branch_stack.shape, bf16)],
        [vmem, anywhere],
        [vmem, anywhere],
        [
            pltpu.VMEM((hops + 1,) + block_shape, bf16),
            pltpu.VMEM((hops,) + block_shape, bf16),
            pltpu.VMEM((hops,) + block_shape, bf16),
        ],
        2 * hops + 1 + model_count - 1,
        1,
    )
    layer_output = (
        layer_input
        + jnp.sum(branch_rows.astype(f32), axis=0)
        + (full_dense_bias + full_down_bias)[None, :]
    )
    key_grads = rotate_back(
        pair_grads[:, :local_width].reshape(group_rows, local_heads, head_dim),
        group_cos,
        group_sin,
    )
    query_back = rotate_back(query_grads, group_cos, group_sin)
    qkv_grads = jnp.concatenate(
        [
            query_back.reshape(group_rows, local_width),
            key_grads.reshape(group_rows, local_width),
            pair_grads[:, local_width:],
        ],
        axis=1,
    ).astype(bf16)
    grad_parts = jnp.concatenate(
        [
            contract_rows(h_attn, qkv_grads).astype(bf16),
            contract_rows(grad_rows, out_flat).astype(bf16),
            contract_rows(h_mlp, hidden_low).astype(bf16),
            contract_rows(grad_rows, activation).astype(bf16),
        ],
        axis=1,
    ).reshape(chip_count, 2, owned, columns)
    attn_input_part = contract_cols(qkv_grads, w_qkv)
    hat_part = (attn_input_part * gain_one + mlp_input_part * gain_two).astype(bf16)
    hat_stack = hat_part.reshape(model_count, tok_dev, model_width)

    def widen(vector, shape, axis, offset):
        return lax.dynamic_update_slice_in_dim(
            jnp.zeros(shape, f32), vector, offset, axis
        ).reshape(fsdp_count, -1)

    qkv_bias_part = jnp.sum(qkv_grads.astype(f32), axis=0)
    small = [
        widen(
            qkv_bias_part.reshape(3, local_heads, head_dim),
            (3, head_count, head_dim),
            1,
            model_rank * local_heads,
        ),
        jnp.sum(cotangent, axis=0).reshape(fsdp_count, -1),
        widen(jnp.sum(hidden_grads, axis=0), (hidden_total,), 0, model_rank * hidden_local),
        jnp.sum(attn_input_part * normed_rows, axis=0).reshape(fsdp_count, -1),
        jnp.sum(attn_input_part, axis=0).reshape(fsdp_count, -1),
        jnp.sum(mlp_input_part * normed_rows, axis=0).reshape(fsdp_count, -1),
        jnp.sum(mlp_input_part, axis=0).reshape(fsdp_count, -1),
    ]
    small_pack = jnp.concatenate(small, axis=1)
    small_width = small_pack.shape[1]
    small_pack = small_pack.reshape(chip_count, 2, 1, small_width)
    grad_shape, small_shape = (owned, columns), (1, small_width)
    grads, small_sums, hat_rows = call(
        functools.partial(close_kernel, chip_count, model_count),
        3,
        (grad_parts, small_pack, hat_stack),
        [(grad_shape, f32), (small_shape, f32), (hat_stack.shape, bf16)],
        [vmem, vmem, anywhere],
        [vmem, vmem, anywhere],
        [
            pltpu.VMEM((chip_count,) + grad_shape, bf16),
            pltpu.VMEM((chip_count - 1,) + grad_shape, bf16),
            pltpu.VMEM((chip_count - 1,) + grad_shape, bf16),
            pltpu.VMEM((chip_count,) + small_shape, f32),
            pltpu.VMEM((chip_count - 1,) + small_shape, f32),
            pltpu.VMEM((chip_count - 1,) + small_shape, f32),
        ],
        2 * (2 * chip_count - 1) + model_count - 1,
        1,
    )
    heavy = grads[:, : 4 * local_width].astype(bf16)
    heavy_all, small_all = call(
        functools.partial(last_kernel, model_count),
        4,
        (heavy, small_sums),
        [((model_count,) + heavy.shape, bf16), ((model_count,) + small_shape, f32)],
        [anywhere] * 2,
        [anywhere] * 2,
        [],
        2 * (model_count - 1),
        2,
    )
    grad_hat = jnp.sum(hat_rows.astype(f32), axis=0)
    input_grad = cotangent + norm_back(grad_hat, normed, inv_std)
    heavy_all = heavy_all.astype(f32)
    grad_qkv_w = (
        heavy_all[:, :, : 3 * local_width]
        .reshape(model_count, owned, 3, local_heads, head_dim)
        .transpose(1, 2, 0, 3, 4)
        .reshape(owned, 3, head_count, head_dim)
    )
    grad_dense_w = (
        heavy_all[:, :, 3 * local_width :].transpose(0, 2, 1).reshape(model_width, owned)
    )
    small_total = jnp.sum(small_all, axis=0)[0]
    final = []
    at = 0
    for piece in small:
        final.append(small_total[at : at + piece.shape[1]])
        at += piece.shape[1]
    return (
        layer_output,
        input_grad,
        grad_qkv_w,
        final[0],
        grad_dense_w,
        final[1],
        final[3],
        final[4],
        final[5],
        final[6],
        grads[:, 4 * local_width : 4 * local_width + hidden_local],
        final[2],
        grads[:, 4 * local_width + hidden_local :],
        final[1],
    )


def solution(mesh):
    placed = (
        P(("fsdp", "mp"), None),
        P(("fsdp", "mp"), None),
        P(),
        P("fsdp"),
        P("fsdp"),
        P("fsdp"),
        P("fsdp"),
        P("fsdp", None, None, None),
        P("fsdp"),
        P(None, "fsdp"),
        P("fsdp"),
        P("fsdp", "mp"),
        P("fsdp"),
        P("fsdp", "mp"),
        P("fsdp"),
    )
    return jax.shard_map(
        on_device,
        mesh=mesh,
        in_specs=placed,
        out_specs=(
            P(("fsdp", "mp"), None),
            P(("fsdp", "mp"), None),
            P("fsdp", None, None, None),
            P("fsdp"),
            P(None, "fsdp"),
            P("fsdp"),
            P("fsdp"),
            P("fsdp"),
            P("fsdp"),
            P("fsdp"),
            P("fsdp", "mp"),
            P("fsdp"),
            P("fsdp", "mp"),
            P("fsdp"),
        ),
        check_vma=False,
    )
```

```python
import functools
import math

import jax
import jax.numpy as jnp
from jax import lax
from jax.experimental import pallas as pl
from jax.experimental.pallas import tpu as pltpu
from jax.sharding import PartitionSpec as P

ROT = 16
SPAN = 16


EPS = 1e-05
NEG_FILL = -1e30


def norm_parts(inputs):
    row_mean = jnp.mean(inputs, axis=-1, keepdims=True)
    centred = inputs - row_mean
    row_var = jnp.mean(centred * centred, axis=-1, keepdims=True)
    inv_std = lax.rsqrt(row_var + EPS)
    return (centred * inv_std, inv_std)


def norm_back(grad_hat, normed, inv_std):
    first_mean = jnp.mean(grad_hat, axis=-1, keepdims=True)
    second_mean = jnp.mean(grad_hat * normed, axis=-1, keepdims=True)
    return inv_std * (grad_hat - first_mean - normed * second_mean)


def gelu_value(pre_act):
    return 0.5 * pre_act * (1.0 + lax.erf(pre_act * (1.0 / math.sqrt(2.0))))


def gelu_slope(pre_act):
    cumulative = 0.5 * (1.0 + lax.erf(pre_act * (1.0 / math.sqrt(2.0))))
    return cumulative + pre_act * jnp.exp(-0.5 * pre_act * pre_act) * (
        1.0 / math.sqrt(2.0 * math.pi)
    )


def rotary_tables(positions):
    half_rot = ROT // 2
    inverse = jnp.exp(jnp.arange(half_rot, dtype=jnp.float32) * (-2.0 * math.log(10000.0) / ROT))
    phase_angle = positions.astype(jnp.float32)[:, None] * inverse[None, :]
    return (jnp.cos(phase_angle)[:, None, :], jnp.sin(phase_angle)[:, None, :])


def rotate(vectors, cosine, sine_table):
    half_rot = ROT // 2
    first_half = vectors[..., :half_rot]
    second_half = vectors[..., half_rot:ROT]
    return jnp.concatenate(
        [
            first_half * cosine - second_half * sine_table,
            second_half * cosine + first_half * sine_table,
            vectors[..., ROT:],
        ],
        axis=-1,
    )


def rotate_back(grads, cosine, sine_table):
    half_rot = ROT // 2
    first_half = grads[..., :half_rot]
    second_half = grads[..., half_rot:ROT]
    return jnp.concatenate(
        [
            first_half * cosine + second_half * sine_table,
            second_half * cosine - first_half * sine_table,
            grads[..., ROT:],
        ],
        axis=-1,
    )


def token_segments(seq_lengths, token_index):
    seq_ends = jnp.cumsum(seq_lengths, dtype=jnp.int32)
    seq_starts = seq_ends - seq_lengths
    segment_ids = jnp.sum(
        (seq_ends[None, :] <= token_index[:, None]).astype(jnp.int32), axis=1, dtype=jnp.int32
    )
    chosen = segment_ids[:, None] == jnp.arange(seq_lengths.shape[0], dtype=jnp.int32)[None, :]
    first_token = jnp.sum(jnp.where(chosen, seq_starts[None, :], 0), axis=1, dtype=jnp.int32)
    return (segment_ids, token_index - first_token)


def contract_rows(left, right):
    return lax.dot_general(
        left, right, (((0,), (0,)), ((), ())), preferred_element_type=jnp.float32
    )


def contract_cols(left, right):
    return lax.dot_general(
        left, right, (((1,), (1,)), ((), ())), preferred_element_type=jnp.float32
    )


def place():
    rank = lax.axis_index("fsdp")
    return rank // 2, rank % 2, lax.axis_index("mp")


def enter(chip_count, model_count):
    chip, core, model = place()
    barrier = pltpu.get_barrier_semaphore()
    peers = []
    if chip_count:
        peers.append((chip * 2 + (1 - core), model))
        for step in range(1, chip_count):
            peers.append((((chip + step) % chip_count) * 2 + core, model))
    for step in range(1, model_count):
        peers.append((chip * 2 + core, (model + step) % model_count))
    for peer in peers:
        pl.semaphore_signal(
            barrier, inc=1, device_id=peer, device_id_type=pl.DeviceIdType.MESH
        )
    pl.semaphore_wait(barrier, len(peers))


class Copies:
    def __init__(self, send, recv, local):
        self.send, self.recv, self.local = send, recv, local
        self.used, self.used_local = 0, 0

    def remote(self, source, target, peer):
        index = self.used
        self.used += 1
        return pltpu.make_async_remote_copy(
            src_ref=source,
            dst_ref=target,
            send_sem=self.send.at[index],
            recv_sem=self.recv.at[index],
            device_id=peer,
            device_id_type=pl.DeviceIdType.MESH,
        )

    def within(self, source, target):
        index = self.used_local
        self.used_local += 1
        return pltpu.make_async_copy(source, target, self.local.at[index])


def model_exchange(copies, source, target, model_count, gather):
    chip, core, model = place()
    started = []
    own = copies.within(source if gather else source.at[model], target.at[model])
    own.start()
    for step in range(1, model_count):
        peer = (model + step) % model_count
        copy = copies.remote(
            source if gather else source.at[peer], target.at[model], (chip * 2 + core, peer)
        )
        copy.start()
        started.append(copy)
    return [own] + started


def gather_start(copies, source, target, chip_count):
    chip, core, model = place()
    rank = chip * 2 + core
    own = copies.within(source, target.at[rank])
    own.start()
    to_pair = copies.remote(source, target.at[rank], (chip * 2 + (1 - core), model))
    to_pair.start()
    far = []
    for step in range(1, chip_count):
        peer = ((chip + step) % chip_count) * 2 + core
        copy = copies.remote(source, target.at[rank], (peer, model))
        copy.start()
        far.append(copy)
    return [own, to_pair], far


def gather_forward(copies, target, far, chip_count):
    chip, core, model = place()
    waits = []
    for step in range(1, chip_count):
        far[step - 1].wait_recv()
        slot = ((chip + chip_count - step) % chip_count) * 2 + core
        copy = copies.remote(target.at[slot], target.at[slot], (chip * 2 + (1 - core), model))
        copy.start()
        waits.append(copy)
    return waits


def open_kernel(chip_count, model_count, w_ref, v_ref, t_ref, w_out, v_out, t_out, s, r, l):
    enter(chip_count, model_count)
    copies = Copies(s, r, l)
    tokens = model_exchange(copies, t_ref, t_out, model_count, True)
    near_v, far_v = gather_start(copies, v_ref, v_out, chip_count)
    near_w, far_w = gather_start(copies, w_ref, w_out, chip_count)
    more = gather_forward(copies, v_out, far_v, chip_count)
    more += gather_forward(copies, w_out, far_w, chip_count)
    for copy in far_v + far_w:
        copy.wait_send()
    for copy in tokens + near_v + near_w + more:
        copy.wait()


def keys_kernel(chip_count, hops, x_ref, out, s, r, l):
    enter(chip_count, 1)
    copies = Copies(s, r, l)
    chip, core, model = place()
    pair = (chip * 2 + (1 - core), model)
    near = copies.remote(x_ref, out.at[0, core], pair)
    near.start()
    far, onward = [], []
    for step in range(1, hops + 1):
        target = ((chip + step) % chip_count) * 2 + core
        far.append(copies.remote(x_ref, out.at[step, core], (target, model)))
        onward.append(copies.remote(out.at[step, core], out.at[step, core], pair))

        @pl.when(chip + step < chip_count)
        def _(copy=far[-1]):
            copy.start()

    for step in range(1, hops + 1):

        @pl.when(chip >= step)
        def _(arrived=far[step - 1], copy=onward[step - 1]):
            arrived.wait_recv()
            copy.start()

    near.wait()
    for step in range(1, hops + 1):

        @pl.when(chip >= step)
        def _(copy=onward[step - 1]):
            copy.wait()

        @pl.when(chip + step < chip_count)
        def _(copy=far[step - 1]):
            copy.wait_send()


def pair_kernel(
    chip_count, model_count, hops, p_ref, b_ref, out, b_out, near_buf, sums, far_buf, s, r, l
):
    enter(chip_count, model_count)
    copies = Copies(s, r, l)
    chip, core, model = place()
    pair = (chip * 2 + (1 - core), model)
    near = [
        copies.remote(p_ref.at[1 - core, step], near_buf.at[step], pair)
        for step in range(hops + 1)
    ]
    for copy in near:
        copy.start()
    branch = model_exchange(copies, b_ref, b_out, model_count, False)
    far = []
    for step in list(range(1, hops + 1)) + [0]:
        near[step].wait_recv()
        total = p_ref[core, step].astype(jnp.float32) + near_buf[step].astype(jnp.float32)
        if step == 0:
            out[...] = total
            continue
        sums[step - 1] = total.astype(sums.dtype)
        target = ((chip + chip_count - step) % chip_count) * 2 + core
        far.append(copies.remote(sums.at[step - 1], far_buf.at[step - 1], (target, model)))

        @pl.when(chip >= step)
        def _(copy=far[-1]):
            copy.start()

    for step in range(1, hops + 1):

        @pl.when(chip + step < chip_count)
        def _(copy=far[step - 1], step=step):
            copy.wait_recv()
            out[...] += far_buf[step - 1].astype(jnp.float32)

    for step in range(1, hops + 1):

        @pl.when(chip >= step)
        def _(copy=far[step - 1]):
            copy.wait_send()

    for copy in near:
        copy.wait_send()
    for copy in branch:
        copy.wait()


def reduce_near(copies, source, near_buf, chip_count):
    chip, core, model = place()
    near = []
    for step in list(range(1, chip_count)) + [0]:
        target = (chip + step) % chip_count
        copy = copies.remote(
            source.at[target, 1 - core], near_buf.at[step], (chip * 2 + (1 - core), model)
        )
        copy.start()
        near.append(copy)
    return near


def reduce_far(copies, source, near_buf, sums, far_buf, out, near, chip_count):
    chip, core, model = place()
    far = []
    for index, step in enumerate(list(range(1, chip_count)) + [0]):
        target = (chip + step) % chip_count
        near[index].wait_recv()
        total = source[target, core].astype(jnp.float32) + near_buf[step].astype(jnp.float32)
        if step == 0:
            out[...] = total
            continue
        sums[step - 1] = total.astype(sums.dtype)
        copy = copies.remote(sums.at[step - 1], far_buf.at[step - 1], (target * 2 + core, model))
        copy.start()
        far.append(copy)
    return far


def reduce_end(out, far_buf, near, far):
    for index, copy in enumerate(far):
        copy.wait_recv()
        out[...] += far_buf[index].astype(jnp.float32)
    for copy in near + far:
        copy.wait_send()


def close_kernel(
    chip_count, model_count, g_ref, v_ref, b_ref, g_out, v_out, b_out,
    g_near, g_sums, g_far, v_near, v_sums, v_far, s, r, l,
):
    enter(chip_count, model_count)
    copies = Copies(s, r, l)
    v_started = reduce_near(copies, v_ref, v_near, chip_count)
    g_started = reduce_near(copies, g_ref, g_near, chip_count)
    branch = model_exchange(copies, b_ref, b_out, model_count, False)
    v_sent = reduce_far(copies, v_ref, v_near, v_sums, v_far, v_out, v_started, chip_count)
    g_sent = reduce_far(copies, g_ref, g_near, g_sums, g_far, g_out, g_started, chip_count)
    reduce_end(v_out, v_far, v_started, v_sent)
    reduce_end(g_out, g_far, g_started, g_sent)
    for copy in branch:
        copy.wait()


def last_kernel(model_count, g_ref, v_ref, g_out, v_out, s, r, l):
    enter(0, model_count)
    copies = Copies(s, r, l)
    started = model_exchange(copies, v_ref, v_out, model_count, True)
    started += model_exchange(copies, g_ref, g_out, model_count, True)
    for copy in started:
        copy.wait()


def over_rows(left, right):
    return lax.dot_general(
        left, right, (((0,), (0,)), ((), ())), preferred_element_type=jnp.float32
    )


def attention_kernel(
    heads, slots, live, q_ref, own_ref, others, h_ref, q_seg, own_seg, key_segs,
    out, q_grads, parts, tops, totals, mixed, lse, delta,
):
    rows, width = q_ref.shape
    head_dim = width // heads
    core = lax.axis_index("fsdp") % 2
    scale = jnp.asarray(1.0 / math.sqrt(head_dim), jnp.bfloat16)

    def columns(value, head, base=0):
        return value[:, base + head * head_dim : base + (head + 1) * head_dim]

    def lines(head):
        return slice(head * head_dim, (head + 1) * head_dim)

    queries = q_ref[...] * scale
    upper = h_ref[...]
    query_segs = q_seg[...]
    own_mask = (own_seg[...] == query_segs) & (
        lax.broadcasted_iota(jnp.int32, (rows, rows), 0)
        <= lax.broadcasted_iota(jnp.int32, (rows, rows), 1)
    )

    def scores_of(block, mask, head):
        return jnp.where(
            mask, contract_cols(columns(block, head), columns(queries, head)), NEG_FILL
        )

    own = own_ref[...]
    for head in range(heads):
        scores = scores_of(own, own_mask, head)
        top = jnp.max(scores, axis=0, keepdims=True)
        weights = jnp.exp(scores - top)
        tops[head] = top
        totals[head] = jnp.sum(weights, axis=0, keepdims=True)
        mixed[lines(head)] = over_rows(
            columns(own, head, width), weights.astype(jnp.bfloat16)
        )

    def forward_slot(index, carried):
        @pl.when(live[index] == 1)
        def _():
            block = others[index]
            mask = key_segs[index] == query_segs
            for head in range(heads):
                scores = scores_of(block, mask, head)
                top = jnp.maximum(tops[head], jnp.max(scores, axis=0, keepdims=True))
                shrink = jnp.exp(tops[head] - top)
                weights = jnp.exp(scores - top)
                tops[head] = top
                totals[head] = totals[head] * shrink + jnp.sum(weights, axis=0, keepdims=True)
                mixed[lines(head)] = mixed[lines(head)] * shrink + over_rows(
                    columns(block, head, width), weights.astype(jnp.bfloat16)
                )

        return carried

    lax.fori_loop(0, slots, forward_slot, 0)
    upper_lines = upper.astype(jnp.float32).T
    for head in range(heads):
        result = (mixed[lines(head)] / totals[head]).astype(jnp.bfloat16).astype(jnp.float32)
        mixed[lines(head)] = result
        lse[head] = tops[head] + jnp.log(totals[head])
        delta[head] = jnp.sum(result * upper_lines[lines(head)], axis=0, keepdims=True)
    out[...] = mixed[...].T.astype(jnp.bfloat16)

    def grads_of(block, mask):
        key_parts, value_parts, query_parts = [], [], []
        for head in range(heads):
            probs = jnp.exp(scores_of(block, mask, head) - lse[head])
            prob_grads = contract_cols(columns(block, head, width), columns(upper, head))
            score_grads = (probs * (prob_grads - delta[head])).astype(jnp.bfloat16)
            query_parts.append(over_rows(columns(block, head), score_grads))
            key_parts.append(
                jnp.dot(score_grads, columns(queries, head), preferred_element_type=jnp.float32)
            )
            value_parts.append(
                jnp.dot(
                    probs.astype(jnp.bfloat16),
                    columns(upper, head),
                    preferred_element_type=jnp.float32,
                )
            )
        both = jnp.concatenate(key_parts + value_parts, axis=1).astype(jnp.bfloat16)
        return both, jnp.concatenate(query_parts, axis=0)

    own_part, first = grads_of(own, own_mask)
    mixed[...] = first

    def backward_slot(index, carried):
        @pl.when(live[index] == 1)
        def _():
            both, more = grads_of(others[index], key_segs[index] == query_segs)
            parts[index % 2, index // 2] = both
            mixed[...] += more

        @pl.when(live[index] != 1)
        def _():
            parts[index % 2, index // 2] = jnp.zeros(own_ref.shape, jnp.bfloat16)

        return carried

    lax.fori_loop(0, slots, backward_slot, 0)
    parts[core, 0] = own_part
    q_grads[...] = (mixed[...] * scale.astype(jnp.float32)).T


def call(kernel, number, operands, outs, spaces, out_spaces, scratch, remote, local):
    return pl.pallas_call(
        kernel,
        out_shape=[jax.ShapeDtypeStruct(shape, dtype) for shape, dtype in outs],
        in_specs=[pl.BlockSpec(memory_space=space) for space in spaces],
        out_specs=[pl.BlockSpec(memory_space=space) for space in out_spaces],
        scratch_shapes=scratch
        + [
            pltpu.SemaphoreType.DMA((remote,)),
            pltpu.SemaphoreType.DMA((remote,)),
            pltpu.SemaphoreType.DMA((max(local, 1),)),
        ],
        compiler_params=pltpu.CompilerParams(collective_id=number, has_side_effects=True),
    )(*operands)


def on_device(
    layer_input,
    cotangent,
    seq_lengths,
    gain_attn,
    beta_attn,
    gain_mlp,
    beta_mlp,
    qkv_weight,
    qkv_bias,
    dense_weight,
    dense_bias,
    up_weight,
    up_bias,
    down_weight,
    down_bias,
):
    fsdp_count = lax.axis_size("fsdp")
    model_count = lax.axis_size("mp")
    chip_count = fsdp_count // 2
    fsdp_rank = lax.axis_index("fsdp")
    model_rank = lax.axis_index("mp")
    chip, core = fsdp_rank // 2, fsdp_rank % 2
    tok_dev, model_width = layer_input.shape
    owned = qkv_weight.shape[0]
    head_count, head_dim = qkv_weight.shape[2:]
    local_heads = head_count // model_count
    local_width = local_heads * head_dim
    hidden_local = up_weight.shape[1]
    hidden_total = hidden_local * model_count
    group_rows = model_count * tok_dev
    key_reach = min(SPAN * group_rows, group_rows * fsdp_count // 2)
    hops = (key_reach // group_rows + 1) // 2
    bf16, f32 = jnp.bfloat16, jnp.float32
    vmem, anywhere = pltpu.VMEM, pl.ANY

    own_qkv = lax.dynamic_slice_in_dim(qkv_weight, model_rank * local_heads, local_heads, 2)
    own_dense = lax.dynamic_slice_in_dim(dense_weight, model_rank * local_width, local_width, 0)
    pack = jnp.concatenate(
        [own_qkv.reshape(owned, 3 * local_width), own_dense.T, up_weight, down_weight], axis=1
    )
    vectors = (qkv_bias, dense_bias, up_bias, down_bias, gain_attn, beta_attn, gain_mlp, beta_mlp)
    vector_pack = jnp.concatenate(vectors).astype(f32)[None, :]
    normed, inv_std = norm_parts(layer_input)
    grad_low = cotangent.astype(bf16)
    token_pack = jnp.concatenate([normed.astype(bf16), grad_low], axis=1)
    columns = pack.shape[1]
    weights, vector_all, token_rows = call(
        functools.partial(open_kernel, chip_count, model_count),
        0,
        (pack, vector_pack, token_pack),
        [
            ((fsdp_count,) + pack.shape, bf16),
            ((fsdp_count,) + vector_pack.shape, f32),
            ((model_count,) + token_pack.shape, bf16),
        ],
        [anywhere] * 3,
        [anywhere] * 3,
        [],
        (model_count - 1) + 2 * (2 * chip_count - 1),
        3,
    )
    weights = weights.reshape(model_width, columns)
    w_qkv = weights[:, : 3 * local_width]
    w_dense = weights[:, 3 * local_width : 4 * local_width]
    w_up = weights[:, 4 * local_width : 4 * local_width + hidden_local]
    w_down = weights[:, 4 * local_width + hidden_local :]
    full = []
    at = 0
    for vector in vectors:
        full.append(vector_all[:, 0, at : at + vector.shape[0]].reshape(-1))
        at += vector.shape[0]
    full_qkv_bias, full_dense_bias, full_up_bias, full_down_bias = full[:4]
    gain_one, shift_one, gain_two, shift_two = full[4:]
    local_qkv_bias = lax.dynamic_slice_in_dim(
        full_qkv_bias.reshape(3, head_count, head_dim), model_rank * local_heads, local_heads, 1
    ).reshape(3 * local_width)
    local_up_bias = lax.dynamic_slice_in_dim(
        full_up_bias, model_rank * hidden_local, hidden_local, 0
    )
    token_rows = token_rows.reshape(group_rows, 2 * model_width)
    normed_rows = token_rows[:, :model_width].astype(f32)
    grad_rows = token_rows[:, model_width:]
    h_attn = (normed_rows * gain_one + shift_one).astype(bf16)
    h_mlp = (normed_rows * gain_two + shift_two).astype(bf16)

    group_index = fsdp_rank * group_rows + jnp.arange(group_rows, dtype=jnp.int32)
    group_seg, group_pos = token_segments(seq_lengths, group_index)
    group_cos, group_sin = rotary_tables(group_pos)
    projected = jnp.dot(h_attn, w_qkv, preferred_element_type=f32) + local_qkv_bias[None, :]
    projected = projected.reshape(group_rows, 3, local_heads, head_dim)
    query_rows = (
        rotate(projected[:, 0], group_cos, group_sin)
        .astype(bf16)
        .reshape(group_rows, local_width)
    )
    own_keys = rotate(projected[:, 1], group_cos, group_sin).astype(bf16)
    own_pair = jnp.concatenate(
        [own_keys.reshape(group_rows, local_width),
         projected[:, 2].astype(bf16).reshape(group_rows, local_width)], axis=1
    )
    (others,) = call(
        functools.partial(keys_kernel, chip_count, hops),
        1,
        (own_pair,),
        [((hops + 1, 2) + own_pair.shape, bf16)],
        [anywhere],
        [anywhere],
        [],
        1 + 2 * hops,
        0,
    )

    pre_act = jnp.dot(h_mlp, w_up, preferred_element_type=f32) + local_up_bias[None, :]
    activation = gelu_value(pre_act).astype(bf16)
    mlp_part = contract_cols(activation, w_down)
    hidden_grads = jnp.dot(grad_rows, w_down, preferred_element_type=f32) * gelu_slope(pre_act)
    hidden_low = hidden_grads.astype(bf16)
    mlp_input_part = contract_cols(hidden_low, w_up)

    slots = 2 * (hops + 1)
    slot_step = jnp.arange(slots, dtype=jnp.int32) // 2
    slot_source = (chip - slot_step) * 2 + jnp.arange(slots, dtype=jnp.int32) % 2
    slot_tokens = (
        slot_source[:, None] * group_rows + jnp.arange(group_rows, dtype=jnp.int32)[None, :]
    )
    slot_segs, unused = token_segments(seq_lengths, slot_tokens.reshape(-1))
    slot_segs = slot_segs.reshape(slots, group_rows)
    live = (
        (slot_source >= 0) & (slot_source < fsdp_rank) & (slot_segs[:, -1] == group_seg[0])
    ).astype(jnp.int32)
    head_grads = jnp.dot(grad_rows, w_dense, preferred_element_type=f32).astype(bf16)
    smem = pltpu.SMEM
    stat = pltpu.VMEM((local_heads, 1, group_rows), f32)
    out_flat, query_grads, part_stack = pl.pallas_call(
        functools.partial(attention_kernel, local_heads, slots),
        out_shape=[
            jax.ShapeDtypeStruct((group_rows, local_width), bf16),
            jax.ShapeDtypeStruct((group_rows, local_width), f32),
            jax.ShapeDtypeStruct((2, hops + 1) + own_pair.shape, bf16),
        ],
        in_specs=[pl.BlockSpec(memory_space=smem)] + [pl.BlockSpec(memory_space=vmem)] * 7,
        out_specs=[pl.BlockSpec(memory_space=vmem)] * 3,
        scratch_shapes=[
            stat, stat, pltpu.VMEM((local_width, group_rows), f32), stat, stat,
        ],
    )(
        live,
        query_rows,
        own_pair,
        others.reshape((slots,) + own_pair.shape),
        head_grads,
        group_seg[None, :],
        group_seg[:, None],
        slot_segs[:, :, None],
    )
    query_grads = query_grads.reshape(group_rows, local_heads, head_dim)
    branch_part = (mlp_part + contract_cols(out_flat, w_dense)).astype(bf16)
    branch_stack = branch_part.reshape(model_count, tok_dev, model_width)
    block_shape = own_pair.shape
    pair_grads, branch_rows = call(
        functools.partial(pair_kernel, chip_count, model_count, hops),
        2,
        (part_stack, branch_stack),
        [(block_shape, f32), (branch_stack.shape, bf16)],
        [vmem, anywhere],
        [vmem, anywhere],
        [
            pltpu.VMEM((hops + 1,) + block_shape, bf16),
            pltpu.VMEM((hops,) + block_shape, bf16),
            pltpu.VMEM((hops,) + block_shape, bf16),
        ],
        2 * hops + 1 + model_count - 1,
        1,
    )
    layer_output = (
        layer_input
        + jnp.sum(branch_rows.astype(f32), axis=0)
        + (full_dense_bias + full_down_bias)[None, :]
    )
    key_grads = rotate_back(
        pair_grads[:, :local_width].reshape(group_rows, local_heads, head_dim),
        group_cos,
        group_sin,
    )
    query_back = rotate_back(query_grads, group_cos, group_sin)
    qkv_grads = jnp.concatenate(
        [
            query_back.reshape(group_rows, local_width),
            key_grads.reshape(group_rows, local_width),
            pair_grads[:, local_width:],
        ],
        axis=1,
    ).astype(bf16)
    grad_parts = jnp.concatenate(
        [
            contract_rows(h_attn, qkv_grads).astype(bf16),
            contract_rows(grad_rows, out_flat).astype(bf16),
            contract_rows(h_mlp, hidden_low).astype(bf16),
            contract_rows(grad_rows, activation).astype(bf16),
        ],
        axis=1,
    ).reshape(chip_count, 2, owned, columns)
    attn_input_part = contract_cols(qkv_grads, w_qkv)
    hat_part = (attn_input_part * gain_one + mlp_input_part * gain_two).astype(bf16)
    hat_stack = hat_part.reshape(model_count, tok_dev, model_width)

    def widen(vector, shape, axis, offset):
        return lax.dynamic_update_slice_in_dim(
            jnp.zeros(shape, f32), vector, offset, axis
        ).reshape(fsdp_count, -1)

    qkv_bias_part = jnp.sum(qkv_grads.astype(f32), axis=0)
    small = [
        widen(
            qkv_bias_part.reshape(3, local_heads, head_dim),
            (3, head_count, head_dim),
            1,
            model_rank * local_heads,
        ),
        jnp.sum(cotangent, axis=0).reshape(fsdp_count, -1),
        widen(jnp.sum(hidden_grads, axis=0), (hidden_total,), 0, model_rank * hidden_local),
        jnp.sum(attn_input_part * normed_rows, axis=0).reshape(fsdp_count, -1),
        jnp.sum(attn_input_part, axis=0).reshape(fsdp_count, -1),
        jnp.sum(mlp_input_part * normed_rows, axis=0).reshape(fsdp_count, -1),
        jnp.sum(mlp_input_part, axis=0).reshape(fsdp_count, -1),
    ]
    small_pack = jnp.concatenate(small, axis=1)
    small_width = small_pack.shape[1]
    small_pack = small_pack.reshape(chip_count, 2, 1, small_width)
    grad_shape, small_shape = (owned, columns), (1, small_width)
    grads, small_sums, hat_rows = call(
        functools.partial(close_kernel, chip_count, model_count),
        3,
        (grad_parts, small_pack, hat_stack),
        [(grad_shape, f32), (small_shape, f32), (hat_stack.shape, bf16)],
        [vmem, vmem, anywhere],
        [vmem, vmem, anywhere],
        [
            pltpu.VMEM((chip_count,) + grad_shape, bf16),
            pltpu.VMEM((chip_count - 1,) + grad_shape, bf16),
            pltpu.VMEM((chip_count - 1,) + grad_shape, bf16),
            pltpu.VMEM((chip_count,) + small_shape, f32),
            pltpu.VMEM((chip_count - 1,) + small_shape, f32),
            pltpu.VMEM((chip_count - 1,) + small_shape, f32),
        ],
        2 * (2 * chip_count - 1) + model_count - 1,
        1,
    )
    heavy = grads[:, : 4 * local_width].astype(bf16)
    heavy_all, small_all = call(
        functools.partial(last_kernel, model_count),
        4,
        (heavy, small_sums),
        [((model_count,) + heavy.shape, bf16), ((model_count,) + small_shape, f32)],
        [anywhere] * 2,
        [anywhere] * 2,
        [],
        2 * (model_count - 1),
        2,
    )
    grad_hat = jnp.sum(hat_rows.astype(f32), axis=0)
    input_grad = cotangent + norm_back(grad_hat, normed, inv_std)
    heavy_all = heavy_all.astype(f32)
    grad_qkv_w = (
        heavy_all[:, :, : 3 * local_width]
        .reshape(model_count, owned, 3, local_heads, head_dim)
        .transpose(1, 2, 0, 3, 4)
        .reshape(owned, 3, head_count, head_dim)
    )
    grad_dense_w = (
        heavy_all[:, :, 3 * local_width :].transpose(0, 2, 1).reshape(model_width, owned)
    )
    small_total = jnp.sum(small_all, axis=0)[0]
    final = []
    at = 0
    for piece in small:
        final.append(small_total[at : at + piece.shape[1]])
        at += piece.shape[1]
    return (
        layer_output,
        input_grad,
        grad_qkv_w,
        final[0],
        grad_dense_w,
        final[1],
        final[3],
        final[4],
        final[5],
        final[6],
        grads[:, 4 * local_width : 4 * local_width + hidden_local],
        final[2],
        grads[:, 4 * local_width + hidden_local :],
        final[1],
    )


def solution(mesh):
    placed = (
        P(("fsdp", "mp"), None),
        P(("fsdp", "mp"), None),
        P(),
        P("fsdp"),
        P("fsdp"),
        P("fsdp"),
        P("fsdp"),
        P("fsdp", None, None, None),
        P("fsdp"),
        P(None, "fsdp"),
        P("fsdp"),
        P("fsdp", "mp"),
        P("fsdp"),
        P("fsdp", "mp"),
        P("fsdp"),
    )
    return jax.shard_map(
        on_device,
        mesh=mesh,
        in_specs=placed,
        out_specs=(
            P(("fsdp", "mp"), None),
            P(("fsdp", "mp"), None),
            P("fsdp", None, None, None),
            P("fsdp"),
            P(None, "fsdp"),
            P("fsdp"),
            P("fsdp"),
            P("fsdp"),
            P("fsdp"),
            P("fsdp"),
            P("fsdp", "mp"),
            P("fsdp"),
            P("fsdp", "mp"),
            P("fsdp"),
        ),
        check_vma=False,
    )
```

```python
import functools
import math

import jax
import jax.numpy as jnp
from jax import lax
from jax.experimental import pallas as pl
from jax.experimental.pallas import tpu as pltpu
from jax.sharding import PartitionSpec as P

ROT = 16
SPAN = 16


EPS = 1e-05
NEG_FILL = -1e30


def norm_parts(inputs):
    row_mean = jnp.mean(inputs, axis=-1, keepdims=True)
    centred = inputs - row_mean
    row_var = jnp.mean(centred * centred, axis=-1, keepdims=True)
    inv_std = lax.rsqrt(row_var + EPS)
    return (centred * inv_std, inv_std)


def norm_back(grad_hat, normed, inv_std):
    first_mean = jnp.mean(grad_hat, axis=-1, keepdims=True)
    second_mean = jnp.mean(grad_hat * normed, axis=-1, keepdims=True)
    return inv_std * (grad_hat - first_mean - normed * second_mean)


def gelu_value(pre_act):
    return 0.5 * pre_act * (1.0 + lax.erf(pre_act * (1.0 / math.sqrt(2.0))))


def gelu_slope(pre_act):
    cumulative = 0.5 * (1.0 + lax.erf(pre_act * (1.0 / math.sqrt(2.0))))
    return cumulative + pre_act * jnp.exp(-0.5 * pre_act * pre_act) * (
        1.0 / math.sqrt(2.0 * math.pi)
    )


def rotary_tables(positions):
    half_rot = ROT // 2
    inverse = jnp.exp(jnp.arange(half_rot, dtype=jnp.float32) * (-2.0 * math.log(10000.0) / ROT))
    phase_angle = positions.astype(jnp.float32)[:, None] * inverse[None, :]
    return (jnp.cos(phase_angle)[:, None, :], jnp.sin(phase_angle)[:, None, :])


def rotate(vectors, cosine, sine_table):
    half_rot = ROT // 2
    first_half = vectors[..., :half_rot]
    second_half = vectors[..., half_rot:ROT]
    return jnp.concatenate(
        [
            first_half * cosine - second_half * sine_table,
            second_half * cosine + first_half * sine_table,
            vectors[..., ROT:],
        ],
        axis=-1,
    )


def rotate_back(grads, cosine, sine_table):
    half_rot = ROT // 2
    first_half = grads[..., :half_rot]
    second_half = grads[..., half_rot:ROT]
    return jnp.concatenate(
        [
            first_half * cosine + second_half * sine_table,
            second_half * cosine - first_half * sine_table,
            grads[..., ROT:],
        ],
        axis=-1,
    )


def token_segments(seq_lengths, token_index):
    seq_ends = jnp.cumsum(seq_lengths, dtype=jnp.int32)
    seq_starts = seq_ends - seq_lengths
    segment_ids = jnp.sum(
        (seq_ends[None, :] <= token_index[:, None]).astype(jnp.int32), axis=1, dtype=jnp.int32
    )
    chosen = segment_ids[:, None] == jnp.arange(seq_lengths.shape[0], dtype=jnp.int32)[None, :]
    first_token = jnp.sum(jnp.where(chosen, seq_starts[None, :], 0), axis=1, dtype=jnp.int32)
    return (segment_ids, token_index - first_token)


def contract_rows(left, right):
    return lax.dot_general(
        left, right, (((0,), (0,)), ((), ())), preferred_element_type=jnp.float32
    )


def contract_cols(left, right):
    return lax.dot_general(
        left, right, (((1,), (1,)), ((), ())), preferred_element_type=jnp.float32
    )


def place():
    rank = lax.axis_index("fsdp")
    return rank // 2, rank % 2, lax.axis_index("mp")


def enter(chip_count, model_count):
    chip, core, model = place()
    barrier = pltpu.get_barrier_semaphore()
    peers = []
    if chip_count:
        peers.append((chip * 2 + (1 - core), model))
        for step in range(1, chip_count):
            peers.append((((chip + step) % chip_count) * 2 + core, model))
    for step in range(1, model_count):
        peers.append((chip * 2 + core, (model + step) % model_count))
    for peer in peers:
        pl.semaphore_signal(
            barrier, inc=1, device_id=peer, device_id_type=pl.DeviceIdType.MESH
        )
    pl.semaphore_wait(barrier, len(peers))


class Copies:
    def __init__(self, send, recv, local):
        self.send, self.recv, self.local = send, recv, local
        self.used, self.used_local = 0, 0

    def remote(self, source, target, peer):
        index = self.used
        self.used += 1
        return pltpu.make_async_remote_copy(
            src_ref=source,
            dst_ref=target,
            send_sem=self.send.at[index],
            recv_sem=self.recv.at[index],
            device_id=peer,
            device_id_type=pl.DeviceIdType.MESH,
        )

    def within(self, source, target):
        index = self.used_local
        self.used_local += 1
        return pltpu.make_async_copy(source, target, self.local.at[index])


def model_exchange(copies, source, target, model_count, gather):
    chip, core, model = place()
    started = []
    own = copies.within(source if gather else source.at[model], target.at[model])
    own.start()
    for step in range(1, model_count):
        peer = (model + step) % model_count
        copy = copies.remote(
            source if gather else source.at[peer], target.at[model], (chip * 2 + core, peer)
        )
        copy.start()
        started.append(copy)
    return [own] + started


def gather_start(copies, source, target, chip_count):
    chip, core, model = place()
    rank = chip * 2 + core
    own = copies.within(source, target.at[rank])
    own.start()
    to_pair = copies.remote(source, target.at[rank], (chip * 2 + (1 - core), model))
    to_pair.start()
    far = []
    for step in range(1, chip_count):
        peer = ((chip + step) % chip_count) * 2 + core
        copy = copies.remote(source, target.at[rank], (peer, model))
        copy.start()
        far.append(copy)
    return [own, to_pair], far


def gather_forward(copies, target, far, chip_count):
    chip, core, model = place()
    waits = []
    for step in range(1, chip_count):
        far[step - 1].wait_recv()
        slot = ((chip + chip_count - step) % chip_count) * 2 + core
        copy = copies.remote(target.at[slot], target.at[slot], (chip * 2 + (1 - core), model))
        copy.start()
        waits.append(copy)
    return waits


def open_kernel(chip_count, model_count, count, *refs):
    sources, t_ref = refs[:count], refs[count]
    targets, t_out = refs[count + 1 : 2 * count + 1], refs[2 * count + 1]
    enter(chip_count, model_count)
    copies = Copies(*refs[2 * count + 2 :])
    waits = model_exchange(copies, t_ref, t_out, model_count, True)
    sent = []
    for source, target in zip(sources, targets):
        near, far = gather_start(copies, source, target, chip_count)
        waits += near
        sent.append(far)
    for target, far in zip(targets, sent):
        waits += gather_forward(copies, target, far, chip_count)
    for far in sent:
        for copy in far:
            copy.wait_send()
    for copy in waits:
        copy.wait()


def keys_kernel(chip_count, model_count, hops, x_ref, t_ref, out, t_out, s, r, l):
    enter(chip_count, model_count)
    copies = Copies(s, r, l)
    tokens = model_exchange(copies, t_ref, t_out, model_count, True)
    chip, core, model = place()
    pair = (chip * 2 + (1 - core), model)
    near = copies.remote(x_ref, out.at[0, core], pair)
    near.start()
    far, onward = [], []
    for step in range(1, hops + 1):
        target = ((chip + step) % chip_count) * 2 + core
        far.append(copies.remote(x_ref, out.at[step, core], (target, model)))
        onward.append(copies.remote(out.at[step, core], out.at[step, core], pair))

        @pl.when(chip + step < chip_count)
        def _(copy=far[-1]):
            copy.start()

    for step in range(1, hops + 1):

        @pl.when(chip >= step)
        def _(arrived=far[step - 1], copy=onward[step - 1]):
            arrived.wait_recv()
            copy.start()

    near.wait()
    for copy in tokens:
        copy.wait()
    for step in range(1, hops + 1):

        @pl.when(chip >= step)
        def _(copy=onward[step - 1]):
            copy.wait()

        @pl.when(chip + step < chip_count)
        def _(copy=far[step - 1]):
            copy.wait_send()


def pair_kernel(
    chip_count, model_count, hops, p_ref, b_ref, out, b_out, near_buf, sums, far_buf, s, r, l
):
    enter(chip_count, model_count)
    copies = Copies(s, r, l)
    chip, core, model = place()
    pair = (chip * 2 + (1 - core), model)
    near = [
        copies.remote(p_ref.at[1 - core, step], near_buf.at[step], pair)
        for step in range(hops + 1)
    ]
    for copy in near:
        copy.start()
    branch = model_exchange(copies, b_ref, b_out, model_count, False)
    far = []
    for step in list(range(1, hops + 1)) + [0]:
        near[step].wait_recv()
        total = p_ref[core, step].astype(jnp.float32) + near_buf[step].astype(jnp.float32)
        if step == 0:
            out[...] = total
            continue
        sums[step - 1] = total.astype(sums.dtype)
        target = ((chip + chip_count - step) % chip_count) * 2 + core
        far.append(copies.remote(sums.at[step - 1], far_buf.at[step - 1], (target, model)))

        @pl.when(chip >= step)
        def _(copy=far[-1]):
            copy.start()

    for step in range(1, hops + 1):

        @pl.when(chip + step < chip_count)
        def _(copy=far[step - 1], step=step):
            copy.wait_recv()
            out[...] += far_buf[step - 1].astype(jnp.float32)

    for step in range(1, hops + 1):

        @pl.when(chip >= step)
        def _(copy=far[step - 1]):
            copy.wait_send()

    for copy in near:
        copy.wait_send()
    for copy in branch:
        copy.wait()


def reduce_near(copies, source, near_buf, chip_count):
    chip, core, model = place()
    near = []
    for step in list(range(1, chip_count)) + [0]:
        target = (chip + step) % chip_count
        copy = copies.remote(
            source.at[target, 1 - core], near_buf.at[step], (chip * 2 + (1 - core), model)
        )
        copy.start()
        near.append(copy)
    return near


def reduce_far(copies, source, near_buf, sums, far_buf, out, near, chip_count):
    chip, core, model = place()
    far = []
    for index, step in enumerate(list(range(1, chip_count)) + [0]):
        target = (chip + step) % chip_count
        near[index].wait_recv()
        total = source[target, core].astype(jnp.float32) + near_buf[step].astype(jnp.float32)
        if step == 0:
            out[...] = total
            continue
        sums[step - 1] = total.astype(sums.dtype)
        copy = copies.remote(sums.at[step - 1], far_buf.at[step - 1], (target * 2 + core, model))
        copy.start()
        far.append(copy)
    return far


def reduce_end(out, far_buf, near, far):
    for index, copy in enumerate(far):
        copy.wait_recv()
        out[...] += far_buf[index].astype(jnp.float32)
    for copy in near + far:
        copy.wait_send()


def close_kernel(chip_count, model_count, count, *refs):
    sources, b_ref = refs[:count], refs[count]
    targets, b_out = refs[count + 1 : 2 * count + 1], refs[2 * count + 1]
    room = refs[2 * count + 2 : 5 * count + 2]
    enter(chip_count, model_count)
    copies = Copies(*refs[5 * count + 2 :])
    started = [
        reduce_near(copies, source, room[3 * at], chip_count)
        for at, source in enumerate(sources)
    ]
    branch = model_exchange(copies, b_ref, b_out, model_count, False)
    sent = [
        reduce_far(
            copies, source, *room[3 * at : 3 * at + 3], targets[at], started[at], chip_count
        )
        for at, source in enumerate(sources)
    ]
    for at, target in enumerate(targets):
        reduce_end(target, room[3 * at + 2], started[at], sent[at])
    for copy in branch:
        copy.wait()


def last_kernel(model_count, count, *refs):
    enter(0, model_count)
    copies = Copies(*refs[2 * count :])
    waits = []
    for source, target in zip(refs[:count], refs[count : 2 * count]):
        waits += model_exchange(copies, source, target, model_count, True)
    for copy in waits:
        copy.wait()


def over_rows(left, right):
    return lax.dot_general(
        left, right, (((0,), (0,)), ((), ())), preferred_element_type=jnp.float32
    )


def attention_kernel(
    heads, slots, live, q_ref, own_ref, others, h_ref, q_seg, own_seg, key_segs,
    out, q_grads, parts, tops, totals, mixed, lse, delta,
):
    rows, width = q_ref.shape
    head_dim = width // heads
    core = lax.axis_index("fsdp") % 2
    scale = jnp.asarray(1.0 / math.sqrt(head_dim), jnp.bfloat16)

    def columns(value, head, base=0):
        return value[:, base + head * head_dim : base + (head + 1) * head_dim]

    def lines(head):
        return slice(head * head_dim, (head + 1) * head_dim)

    queries = q_ref[...] * scale
    upper = h_ref[...]
    query_segs = q_seg[...]
    own_mask = (own_seg[...] == query_segs) & (
        lax.broadcasted_iota(jnp.int32, (rows, rows), 0)
        <= lax.broadcasted_iota(jnp.int32, (rows, rows), 1)
    )

    def scores_of(block, mask, head):
        return jnp.where(
            mask, contract_cols(columns(block, head), columns(queries, head)), NEG_FILL
        )

    own = own_ref[...]
    for head in range(heads):
        scores = scores_of(own, own_mask, head)
        top = jnp.max(scores, axis=0, keepdims=True)
        weights = jnp.exp(scores - top)
        tops[head] = top
        totals[head] = jnp.sum(weights, axis=0, keepdims=True)
        mixed[lines(head)] = over_rows(
            columns(own, head, width), weights.astype(jnp.bfloat16)
        )

    def forward_slot(index, carried):
        @pl.when(live[index] == 1)
        def _():
            block = others[index]
            mask = key_segs[index] == query_segs
            for head in range(heads):
                scores = scores_of(block, mask, head)
                top = jnp.maximum(tops[head], jnp.max(scores, axis=0, keepdims=True))
                shrink = jnp.exp(tops[head] - top)
                weights = jnp.exp(scores - top)
                tops[head] = top
                totals[head] = totals[head] * shrink + jnp.sum(weights, axis=0, keepdims=True)
                mixed[lines(head)] = mixed[lines(head)] * shrink + over_rows(
                    columns(block, head, width), weights.astype(jnp.bfloat16)
                )

        return carried

    lax.fori_loop(0, slots, forward_slot, 0)
    upper_lines = upper.astype(jnp.float32).T
    for head in range(heads):
        result = (mixed[lines(head)] / totals[head]).astype(jnp.bfloat16).astype(jnp.float32)
        mixed[lines(head)] = result
        lse[head] = tops[head] + jnp.log(totals[head])
        delta[head] = jnp.sum(result * upper_lines[lines(head)], axis=0, keepdims=True)
    out[...] = mixed[...].T.astype(jnp.bfloat16)

    def grads_of(block, mask):
        key_parts, value_parts, query_parts = [], [], []
        for head in range(heads):
            probs = jnp.exp(scores_of(block, mask, head) - lse[head])
            prob_grads = contract_cols(columns(block, head, width), columns(upper, head))
            score_grads = (probs * (prob_grads - delta[head])).astype(jnp.bfloat16)
            query_parts.append(over_rows(columns(block, head), score_grads))
            key_parts.append(
                jnp.dot(score_grads, columns(queries, head), preferred_element_type=jnp.float32)
            )
            value_parts.append(
                jnp.dot(
                    probs.astype(jnp.bfloat16),
                    columns(upper, head),
                    preferred_element_type=jnp.float32,
                )
            )
        both = jnp.concatenate(key_parts + value_parts, axis=1).astype(jnp.bfloat16)
        return both, jnp.concatenate(query_parts, axis=0)

    own_part, first = grads_of(own, own_mask)
    mixed[...] = first

    def backward_slot(index, carried):
        @pl.when(live[index] == 1)
        def _():
            both, more = grads_of(others[index], key_segs[index] == query_segs)
            parts[index % 2, index // 2] = both
            mixed[...] += more

        @pl.when(live[index] != 1)
        def _():
            parts[index % 2, index // 2] = jnp.zeros(own_ref.shape, jnp.bfloat16)

        return carried

    lax.fori_loop(0, slots, backward_slot, 0)
    parts[core, 0] = own_part
    q_grads[...] = (mixed[...] * scale.astype(jnp.float32)).T


def call(kernel, number, operands, outs, spaces, out_spaces, scratch, remote, local):
    return pl.pallas_call(
        kernel,
        out_shape=[jax.ShapeDtypeStruct(shape, dtype) for shape, dtype in outs],
        in_specs=[pl.BlockSpec(memory_space=space) for space in spaces],
        out_specs=[pl.BlockSpec(memory_space=space) for space in out_spaces],
        scratch_shapes=scratch
        + [
            pltpu.SemaphoreType.DMA((remote,)),
            pltpu.SemaphoreType.DMA((remote,)),
            pltpu.SemaphoreType.DMA((max(local, 1),)),
        ],
        compiler_params=pltpu.CompilerParams(collective_id=number, has_side_effects=True),
    )(*operands)


def on_device(
    layer_input,
    cotangent,
    seq_lengths,
    gain_attn,
    beta_attn,
    gain_mlp,
    beta_mlp,
    qkv_weight,
    qkv_bias,
    dense_weight,
    dense_bias,
    up_weight,
    up_bias,
    down_weight,
    down_bias,
):
    fsdp_count = lax.axis_size("fsdp")
    model_count = lax.axis_size("mp")
    chip_count = fsdp_count // 2
    fsdp_rank = lax.axis_index("fsdp")
    model_rank = lax.axis_index("mp")
    chip, core = fsdp_rank // 2, fsdp_rank % 2
    tok_dev, model_width = layer_input.shape
    owned = qkv_weight.shape[0]
    head_count, head_dim = qkv_weight.shape[2:]
    local_heads = head_count // model_count
    local_width = local_heads * head_dim
    hidden_local = up_weight.shape[1]
    hidden_total = hidden_local * model_count
    group_rows = model_count * tok_dev
    key_reach = min(SPAN * group_rows, group_rows * fsdp_count // 2)
    hops = (key_reach // group_rows + 1) // 2
    bf16, f32 = jnp.bfloat16, jnp.float32
    vmem, anywhere = pltpu.VMEM, pl.ANY

    own_qkv = lax.dynamic_slice_in_dim(qkv_weight, model_rank * local_heads, local_heads, 2)
    own_dense = lax.dynamic_slice_in_dim(dense_weight, model_rank * local_width, local_width, 0)
    vectors = (qkv_bias, dense_bias, up_bias, down_bias, gain_attn, beta_attn, gain_mlp, beta_mlp)
    vector_pack = jnp.concatenate(vectors).astype(f32)[None, :]
    normed, inv_std = norm_parts(layer_input)
    grad_low = cotangent.astype(bf16)
    normed_low = normed.astype(bf16)
    owned_parts = (
        vector_pack,
        own_qkv.reshape(owned, 3 * local_width),
        up_weight,
        own_dense.T,
        down_weight,
    )
    vector_all, w_qkv, w_up, w_dense, w_down, normed_rows = call(
        functools.partial(open_kernel, chip_count, model_count, len(owned_parts)),
        0,
        owned_parts + (normed_low,),
        [((fsdp_count,) + part.shape, part.dtype) for part in owned_parts]
        + [((model_count,) + normed_low.shape, bf16)],
        [anywhere] * (len(owned_parts) + 1),
        [anywhere] * (len(owned_parts) + 1),
        [],
        (model_count - 1) + len(owned_parts) * (2 * chip_count - 1),
        len(owned_parts) + 1,
    )
    w_qkv, w_up, w_dense, w_down = (
        part.reshape(model_width, part.shape[2]) for part in (w_qkv, w_up, w_dense, w_down)
    )
    full = []
    at = 0
    for vector in vectors:
        full.append(vector_all[:, 0, at : at + vector.shape[0]].reshape(-1))
        at += vector.shape[0]
    full_qkv_bias, full_dense_bias, full_up_bias, full_down_bias = full[:4]
    gain_one, shift_one, gain_two, shift_two = full[4:]
    local_qkv_bias = lax.dynamic_slice_in_dim(
        full_qkv_bias.reshape(3, head_count, head_dim), model_rank * local_heads, local_heads, 1
    ).reshape(3 * local_width)
    local_up_bias = lax.dynamic_slice_in_dim(
        full_up_bias, model_rank * hidden_local, hidden_local, 0
    )
    normed_rows = normed_rows.reshape(group_rows, model_width).astype(f32)
    h_attn = (normed_rows * gain_one + shift_one).astype(bf16)
    h_mlp = (normed_rows * gain_two + shift_two).astype(bf16)

    group_index = fsdp_rank * group_rows + jnp.arange(group_rows, dtype=jnp.int32)
    group_seg, group_pos = token_segments(seq_lengths, group_index)
    group_cos, group_sin = rotary_tables(group_pos)
    projected = jnp.dot(h_attn, w_qkv, preferred_element_type=f32) + local_qkv_bias[None, :]
    projected = projected.reshape(group_rows, 3, local_heads, head_dim)
    query_rows = (
        rotate(projected[:, 0], group_cos, group_sin)
        .astype(bf16)
        .reshape(group_rows, local_width)
    )
    own_keys = rotate(projected[:, 1], group_cos, group_sin).astype(bf16)
    own_pair = jnp.concatenate(
        [own_keys.reshape(group_rows, local_width),
         projected[:, 2].astype(bf16).reshape(group_rows, local_width)], axis=1
    )
    others, grad_rows = call(
        functools.partial(keys_kernel, chip_count, model_count, hops),
        1,
        (own_pair, grad_low),
        [((hops + 1, 2) + own_pair.shape, bf16), ((model_count,) + grad_low.shape, bf16)],
        [anywhere] * 2,
        [anywhere] * 2,
        [],
        1 + 2 * hops + model_count - 1,
        1,
    )
    grad_rows = grad_rows.reshape(group_rows, model_width)

    pre_act = jnp.dot(h_mlp, w_up, preferred_element_type=f32) + local_up_bias[None, :]
    activation = gelu_value(pre_act).astype(bf16)
    mlp_part = contract_cols(activation, w_down)
    hidden_grads = jnp.dot(grad_rows, w_down, preferred_element_type=f32) * gelu_slope(pre_act)
    hidden_low = hidden_grads.astype(bf16)
    mlp_input_part = contract_cols(hidden_low, w_up)

    slots = 2 * (hops + 1)
    slot_step = jnp.arange(slots, dtype=jnp.int32) // 2
    slot_source = (chip - slot_step) * 2 + jnp.arange(slots, dtype=jnp.int32) % 2
    slot_tokens = (
        slot_source[:, None] * group_rows + jnp.arange(group_rows, dtype=jnp.int32)[None, :]
    )
    slot_segs, unused = token_segments(seq_lengths, slot_tokens.reshape(-1))
    slot_segs = slot_segs.reshape(slots, group_rows)
    live = (
        (slot_source >= 0) & (slot_source < fsdp_rank) & (slot_segs[:, -1] == group_seg[0])
    ).astype(jnp.int32)
    head_grads = jnp.dot(grad_rows, w_dense, preferred_element_type=f32).astype(bf16)
    smem = pltpu.SMEM
    stat = pltpu.VMEM((local_heads, 1, group_rows), f32)
    out_flat, query_grads, part_stack = pl.pallas_call(
        functools.partial(attention_kernel, local_heads, slots),
        out_shape=[
            jax.ShapeDtypeStruct((group_rows, local_width), bf16),
            jax.ShapeDtypeStruct((group_rows, local_width), f32),
            jax.ShapeDtypeStruct((2, hops + 1) + own_pair.shape, bf16),
        ],
        in_specs=[pl.BlockSpec(memory_space=smem)] + [pl.BlockSpec(memory_space=vmem)] * 7,
        out_specs=[pl.BlockSpec(memory_space=vmem)] * 3,
        scratch_shapes=[
            stat, stat, pltpu.VMEM((local_width, group_rows), f32), stat, stat,
        ],
    )(
        live,
        query_rows,
        own_pair,
        others.reshape((slots,) + own_pair.shape),
        head_grads,
        group_seg[None, :],
        group_seg[:, None],
        slot_segs[:, :, None],
    )
    query_grads = query_grads.reshape(group_rows, local_heads, head_dim)
    branch_part = (mlp_part + contract_cols(out_flat, w_dense)).astype(bf16)
    branch_stack = branch_part.reshape(model_count, tok_dev, model_width)
    block_shape = own_pair.shape
    pair_grads, branch_rows = call(
        functools.partial(pair_kernel, chip_count, model_count, hops),
        2,
        (part_stack, branch_stack),
        [(block_shape, f32), (branch_stack.shape, bf16)],
        [vmem, anywhere],
        [vmem, anywhere],
        [
            pltpu.VMEM((hops + 1,) + block_shape, bf16),
            pltpu.VMEM((hops,) + block_shape, bf16),
            pltpu.VMEM((hops,) + block_shape, bf16),
        ],
        2 * hops + 1 + model_count - 1,
        1,
    )
    layer_output = (
        layer_input
        + jnp.sum(branch_rows.astype(f32), axis=0)
        + (full_dense_bias + full_down_bias)[None, :]
    )
    key_grads = rotate_back(
        pair_grads[:, :local_width].reshape(group_rows, local_heads, head_dim),
        group_cos,
        group_sin,
    )
    query_back = rotate_back(query_grads, group_cos, group_sin)
    qkv_grads = jnp.concatenate(
        [
            query_back.reshape(group_rows, local_width),
            key_grads.reshape(group_rows, local_width),
            pair_grads[:, local_width:],
        ],
        axis=1,
    ).astype(bf16)
    grad_parts = tuple(
        part.astype(bf16).reshape(chip_count, 2, owned, part.shape[1])
        for part in (
            contract_rows(h_mlp, hidden_low),
            contract_rows(grad_rows, activation),
            contract_rows(grad_rows, out_flat),
            contract_rows(h_attn, qkv_grads),
        )
    )
    attn_input_part = contract_cols(qkv_grads, w_qkv)
    hat_part = (attn_input_part * gain_one + mlp_input_part * gain_two).astype(bf16)
    hat_stack = hat_part.reshape(model_count, tok_dev, model_width)

    def widen(vector, shape, axis, offset):
        return lax.dynamic_update_slice_in_dim(
            jnp.zeros(shape, f32), vector, offset, axis
        ).reshape(fsdp_count, -1)

    qkv_bias_part = jnp.sum(qkv_grads.astype(f32), axis=0)
    small = [
        widen(
            qkv_bias_part.reshape(3, local_heads, head_dim),
            (3, head_count, head_dim),
            1,
            model_rank * local_heads,
        ),
        jnp.sum(cotangent, axis=0).reshape(fsdp_count, -1),
        widen(jnp.sum(hidden_grads, axis=0), (hidden_total,), 0, model_rank * hidden_local),
        jnp.sum(attn_input_part * normed_rows, axis=0).reshape(fsdp_count, -1),
        jnp.sum(attn_input_part, axis=0).reshape(fsdp_count, -1),
        jnp.sum(mlp_input_part * normed_rows, axis=0).reshape(fsdp_count, -1),
        jnp.sum(mlp_input_part, axis=0).reshape(fsdp_count, -1),
    ]
    small_pack = jnp.concatenate(small, axis=1)
    small_width = small_pack.shape[1]
    small_pack = small_pack.reshape(chip_count, 2, 1, small_width)
    summed = (small_pack,) + grad_parts
    small_sums, grad_up_w, grad_down_w, dense_sums, qkv_sums, hat_rows = call(
        functools.partial(close_kernel, chip_count, model_count, len(summed)),
        3,
        summed + (hat_stack,),
        [(part.shape[2:], f32) for part in summed] + [(hat_stack.shape, bf16)],
        [vmem] * len(summed) + [anywhere],
        [vmem] * len(summed) + [anywhere],
        [
            pltpu.VMEM((slots_of,) + part.shape[2:], part.dtype)
            for part in summed
            for slots_of in (chip_count, chip_count - 1, chip_count - 1)
        ],
        len(summed) * (2 * chip_count - 1) + model_count - 1,
        1,
    )
    shared = (small_sums, dense_sums.astype(bf16), qkv_sums.astype(bf16))
    small_all, dense_all, qkv_all = call(
        functools.partial(last_kernel, model_count, len(shared)),
        4,
        shared,
        [((model_count,) + part.shape, part.dtype) for part in shared],
        [anywhere] * len(shared),
        [anywhere] * len(shared),
        [],
        len(shared) * (model_count - 1),
        len(shared),
    )
    grad_hat = jnp.sum(hat_rows.astype(f32), axis=0)
    input_grad = cotangent + norm_back(grad_hat, normed, inv_std)
    grad_qkv_w = (
        qkv_all.astype(f32)
        .reshape(model_count, owned, 3, local_heads, head_dim)
        .transpose(1, 2, 0, 3, 4)
        .reshape(owned, 3, head_count, head_dim)
    )
    grad_dense_w = dense_all.astype(f32).transpose(0, 2, 1).reshape(model_width, owned)
    small_total = jnp.sum(small_all, axis=0)[0]
    final = []
    at = 0
    for piece in small:
        final.append(small_total[at : at + piece.shape[1]])
        at += piece.shape[1]
    return (
        layer_output,
        input_grad,
        grad_qkv_w,
        final[0],
        grad_dense_w,
        final[1],
        final[3],
        final[4],
        final[5],
        final[6],
        grad_up_w,
        final[2],
        grad_down_w,
        final[1],
    )


def solution(mesh):
    placed = (
        P(("fsdp", "mp"), None),
        P(("fsdp", "mp"), None),
        P(),
        P("fsdp"),
        P("fsdp"),
        P("fsdp"),
        P("fsdp"),
        P("fsdp", None, None, None),
        P("fsdp"),
        P(None, "fsdp"),
        P("fsdp"),
        P("fsdp", "mp"),
        P("fsdp"),
        P("fsdp", "mp"),
        P("fsdp"),
    )
    return jax.shard_map(
        on_device,
        mesh=mesh,
        in_specs=placed,
        out_specs=(
            P(("fsdp", "mp"), None),
            P(("fsdp", "mp"), None),
            P("fsdp", None, None, None),
            P("fsdp"),
            P(None, "fsdp"),
            P("fsdp"),
            P("fsdp"),
            P("fsdp"),
            P("fsdp"),
            P("fsdp"),
            P("fsdp", "mp"),
            P("fsdp"),
            P("fsdp", "mp"),
            P("fsdp"),
        ),
        check_vma=False,
    )
```
